32 devices in a mesh: tm: 8 (over z, x), rows: 4 (over y, core).
Axes of the slice: x: 2, y: 2, z: 4, core: 2. Of those that a mesh axis runs over, the one named last changes fastest.
Arguments:
- drift_blocks: bfloat16 [128, 4, 128, 128], P('rows'), may hold values from -0.1875 to 0.1875
- drift_cols: int32 [128, 4], P('rows'), may hold values from 0 to 127
- control_blocks: bfloat16 [4, 128, 128, 128], P(None, 'rows'), may hold values from -0.1875 to 0.1875
- control_cols: int32 [4, 128], P(None, 'rows'), may hold values from 0 to 127
- controls: float32 [4, 40, 8], P(None, 'tm'), may hold values from -4 to 4
- shooting_states: bfloat16 [8, 8, 16384], P('tm', None, 'rows'), may hold values from -6 to 6
- targets: bfloat16 [40, 8, 16384], P('tm', None, 'rows'), may hold values from -6 to 6
Outputs:
- grad_shooting: float32 [8, 8, 16384], P('tm', None, 'rows')
- grad_controls: float32 [4, 40, 8], P(None, 'tm')
- grad_drift: float32 [128, 65536], P('rows', 'tm')
- grad_control_ops: float32 [4, 128, 16384], P(None, 'rows', 'tm')
The draws below stay inside these ranges and needn't reach their ends.
Inputs may be any that keep to these rules, and one draw needn't show every extreme that they name: `drift_cols`: block column index of each stored drift block; several stored blocks may share a column. `control_cols`: block column index of each stored control block.
All inputs are finite; a program needn't handle non-finite values.
Results may differ from the reference program's by a relative error of at most 0.02.
Values may be sent and summed in bfloat16 or wider, within the bound.
A program may use at most 128 MiB of HBM per device.

```python
import jax
import jax.numpy as jnp
from jax import lax

NL = 16384
BS = 128
NB = 128
K = 4
NU = 4
S = 8
L = 5
NC = 8
H = 40


def set_ends(drawn, key, least, largest):
    shape = drawn.shape
    spot = [jax.random.randint(jax.random.fold_in(key, axis), (), 0, shape[axis]) for axis in range(len(shape))]
    drawn = drawn.at[tuple(spot)].set(least)
    longest = shape.index(max(shape))
    spot[longest] = (spot[longest] + 1) % shape[longest]
    return drawn.at[tuple(spot)].set(largest)


def steps_of(stream_key, shape, split, low, top_value):
    level = 1.0
    for dim, shards_of in split:
        steps = jax.random.uniform(jax.random.fold_in(jax.random.fold_in(stream_key, 6), dim), (shards_of,), jnp.float32, low / len(split), top_value / len(split))
        level = level * jnp.repeat(jnp.exp(steps), shape[dim] // shards_of).reshape((-1,) + (1,) * (len(shape) - 1 - dim))
    return level


def gaussian(own_key, shape, deviation, bound, cuts=(), held_as=jnp.bfloat16):
    drawn = deviation * jax.random.normal(own_key, shape, jnp.float32)
    if cuts:
        drawn = drawn * steps_of(own_key, shape, cuts, -0.22, 0.18)
    return jnp.clip(drawn, -bound, bound).astype(held_as)


def setup_inputs(seed: int = 0) -> dict:
    key_of = jax.random.split(jax.random.key(seed), 8)
    return {
        "drift_blocks": gaussian(key_of[0], (NB, K, BS, BS), (2 * K * BS) ** -0.5, 0.1875, ((0, 4),)),
        "drift_cols": set_ends(jax.random.randint(key_of[1], (NB, K), 0, NB), jax.random.fold_in(key_of[1], 1), 0, NB - 1).astype(jnp.int32),
        "control_blocks": gaussian(key_of[2], (NU, NB, BS, BS), (2 * BS * NU) ** -0.5, 0.1875, ((1, 4),)),
        "control_cols": set_ends(jax.random.randint(key_of[3], (NU, NB), 0, NB), jax.random.fold_in(key_of[3], 1), 0, NB - 1).astype(jnp.int32),
        "controls": gaussian(key_of[4], (NU, H, S), 1.0, 4.0, ((1, 8),), jnp.float32),
        "shooting_states": gaussian(key_of[5], (NC, S, NL), 1.0, 6.0, ((0, 8), (2, 4))),
        "targets": gaussian(key_of[6], (H, S, NL), 1.0, 6.0, ((0, 8), (2, 4))),
    }


defect_weight = 2.0


def to_half(value):
    return lax.optimization_barrier(value.astype(jnp.bfloat16))


def step_terms(state_panel, drift_blocks, drift_cols, control_blocks, control_cols):
    blocks = state_panel.reshape(S, NB, BS).astype(jnp.float32)
    picked = blocks[:, drift_cols]
    drift_out = jnp.einsum('snki,nkoi->sno', picked, drift_blocks.astype(jnp.float32))
    control_picked = blocks[:, control_cols]
    control_out = jnp.einsum('sjni,jnoi->sjno', control_picked, control_blocks.astype(jnp.float32))
    return picked, drift_out, control_picked, control_out


def forward_group(first_panel, group_inputs, operators):
    panels = [first_panel]
    state_panel = first_panel
    for position in range(L):
        picked, drift_out, control_picked, control_out = step_terms(state_panel, *operators)
        weights = group_inputs[:, position].T[:, :, None, None]
        mixed = drift_out + jnp.sum(weights * control_out, axis=1)
        state_panel = to_half(mixed.reshape(S, NL))
        panels.append(state_panel)
    return panels


def reference(drift_blocks, drift_cols, control_blocks, control_cols, controls, shooting_states, targets):
    operators = (drift_blocks, drift_cols, control_blocks, control_cols)
    indices = jnp.arange(NC, dtype=jnp.int32)

    def group_controls(group_index):
        return lax.dynamic_slice_in_dim(controls, (group_index * L).astype(jnp.int32), L, 1)

    def end_of(group_index):
        return forward_group(shooting_states[group_index], group_controls(group_index), operators)[-1]

    group_ends = lax.map(end_of, indices)

    def backward(carry, group_index):
        drift_sum, control_sum = carry
        group_inputs = group_controls(group_index)
        group_targets = lax.dynamic_slice_in_dim(targets, (group_index * L).astype(jnp.int32), L, 0)
        panels = forward_group(shooting_states[group_index], group_inputs, operators)
        next_start = shooting_states[jnp.minimum(group_index + 1, NC - 1)].astype(jnp.float32)
        prev_end = group_ends[jnp.maximum(group_index - 1, 0)].astype(jnp.float32)
        group_end = panels[-1].astype(jnp.float32)
        defect = jnp.where(group_index < NC - 1, next_start - group_end, 0.0)
        prev_defect = jnp.where(group_index > 0, shooting_states[group_index].astype(jnp.float32) - prev_end, 0.0)
        adjoint = group_end - group_targets[L - 1].astype(jnp.float32) - defect_weight * defect
        input_grads = [None] * L
        for position in reversed(range(L)):
            adjoint_half = to_half(adjoint).astype(jnp.float32)
            picked, drift_out, control_picked, control_out = step_terms(panels[position], *operators)
            mu_blocks = adjoint_half.reshape(S, NB, BS)
            weights = group_inputs[:, position].T[:, :, None, None]
            input_grads[position] = jnp.sum(mu_blocks[:, None] * control_out, axis=(2, 3)).T
            drift_sum = drift_sum + jnp.einsum('sno,snki->nkoi', mu_blocks, picked)
            weighted = to_half(mu_blocks[:, None] * weights).astype(jnp.float32)
            control_sum = control_sum + jnp.einsum('sjno,sjni->jnoi', weighted, control_picked)
            drift_back = jnp.einsum('sno,nkoi->snki', mu_blocks, drift_blocks.astype(jnp.float32))
            control_back = jnp.einsum('sno,jnoi->sjni', mu_blocks, control_blocks.astype(jnp.float32)) * weights
            spread = jnp.zeros((S, NB, BS), jnp.float32)
            spread = spread.at[:, drift_cols].add(drift_back).at[:, control_cols].add(control_back)
            adjoint = spread.reshape(S, NL)
            if position > 0:
                adjoint = adjoint + panels[position].astype(jnp.float32) - group_targets[position - 1].astype(jnp.float32)
        grad_shoot = adjoint + defect_weight * prev_defect
        return (drift_sum, control_sum), (grad_shoot, jnp.stack(input_grads, 1))

    start = (jnp.zeros((NB, K, BS, BS), jnp.float32), jnp.zeros((NU, NB, BS, BS), jnp.float32))
    (drift_sum, control_sum), (grad_shooting, input_grads) = lax.scan(backward, start, indices)
    grad_controls = jnp.transpose(input_grads, (1, 0, 2, 3)).reshape(NU, H, S) * (NL ** -0.5)
    grad_scale = (S * H) ** -0.5
    grad_drift = drift_sum.reshape(NB, K * BS * BS) * grad_scale
    grad_control_ops = control_sum.reshape(NU, NB, BS * BS) * grad_scale
    return grad_shooting, grad_controls, grad_drift, grad_control_ops
```

```python
import jax
import jax.numpy as jnp
from jax import lax
from jax.experimental import pallas as pl
from jax.experimental.pallas import tpu as pltpu
from jax.sharding import PartitionSpec as P

defect_weight = 2.0


def passed_along(value, axis, by):
    count = lax.axis_size(axis)
    pairs = [(i, i + by) for i in range(count) if 0 <= i + by < count]
    return lax.ppermute(value, axis, pairs)


def step_terms(gathered, block_width, drift_blocks, drift_cols, control_blocks, control_cols):
    blocks = gathered.reshape(gathered.shape[0], -1, block_width)
    total = jnp.arange(blocks.shape[1])
    drift_hits = (drift_cols[..., None] == total).astype(jnp.bfloat16)
    control_hits = (control_cols[..., None] == total).astype(jnp.bfloat16)
    picked = jnp.einsum(
        "nkb,sbi->snki", drift_hits, blocks, preferred_element_type=jnp.float32
    ).astype(jnp.bfloat16)
    drift_out = jnp.einsum(
        "snki,nkoi->sno", picked, drift_blocks, preferred_element_type=jnp.float32
    )
    control_picked = jnp.einsum(
        "jnb,sbi->sjni", control_hits, blocks, preferred_element_type=jnp.float32
    ).astype(jnp.bfloat16)
    control_out = jnp.einsum(
        "sjni,jnoi->sjno", control_picked, control_blocks, preferred_element_type=jnp.float32
    )
    return (picked, drift_out, control_picked, control_out)


def general(
    drift_blocks, drift_cols, control_blocks, control_cols, controls, shooting_states, targets
):
    block_width = drift_blocks.shape[-1]
    scenarios = shooting_states.shape[1]
    local_rows = shooting_states.shape[2]
    horizon_steps = targets.shape[0]
    group_count = lax.axis_size("tm")
    group_index = lax.axis_index("tm")
    total_blocks = drift_blocks.shape[0] * lax.axis_size("rows")
    lifted_total = local_rows * lax.axis_size("rows")
    operators = (drift_blocks, drift_cols, control_blocks, control_cols)
    row_count = lax.axis_size("rows")
    targets_of = jnp.concatenate([drift_cols.reshape(-1), control_cols.reshape(-1)])
    hits = (targets_of[:, None] == jnp.arange(total_blocks)[None]).astype(jnp.bfloat16)
    first_panel = shooting_states[0]
    panels = [first_panel]
    stored = []
    state_panel = first_panel
    for position in range(horizon_steps):
        gathered = lax.all_gather(state_panel, "rows", axis=1, tiled=True)
        step_parts = step_terms(gathered, block_width, *operators)
        stored.append(step_parts)
        weights = controls[:, position].T[:, :, None, None]
        mixed = step_parts[1] + jnp.sum(weights * step_parts[3], axis=1)
        state_panel = mixed.reshape(scenarios, local_rows).astype(jnp.bfloat16)
        panels.append(state_panel)
    group_end = panels[-1]
    next_start = passed_along(first_panel, "tm", -1)
    prev_end = passed_along(group_end, "tm", 1)
    end_wide = group_end.astype(jnp.float32)
    defect = jnp.where(
        group_index < group_count - 1, next_start.astype(jnp.float32) - end_wide, 0.0
    )
    prev_defect = jnp.where(
        group_index > 0, first_panel.astype(jnp.float32) - prev_end.astype(jnp.float32), 0.0
    )
    adjoint = end_wide - targets[horizon_steps - 1].astype(jnp.float32) - defect_weight * defect
    input_grads = [None] * horizon_steps
    mu_list = []
    picked_list = []
    weighted_list = []
    control_picked_list = []
    for position in reversed(range(horizon_steps)):
        adjoint_half = adjoint.astype(jnp.bfloat16)
        picked, drift_out, control_picked, control_out = stored[position]
        mu_blocks = adjoint_half.reshape(scenarios, -1, block_width)
        mu_wide = mu_blocks.astype(jnp.float32)
        weights = controls[:, position].T[:, :, None, None]
        input_grads[position] = jnp.sum(mu_wide[:, None] * control_out, axis=(2, 3)).T
        weighted = (mu_wide[:, None] * weights).astype(jnp.bfloat16)
        mu_list.append(mu_blocks)
        picked_list.append(picked)
        weighted_list.append(weighted)
        control_picked_list.append(control_picked)
        drift_back = jnp.einsum(
            "sno,nkoi->snki", mu_blocks, drift_blocks, preferred_element_type=jnp.float32
        )
        control_back = (
            jnp.einsum(
                "sno,jnoi->sjni", mu_blocks, control_blocks, preferred_element_type=jnp.float32
            )
            * weights
        )
        terms = jnp.concatenate(
            [
                drift_back.reshape(scenarios, -1, block_width),
                control_back.reshape(scenarios, -1, block_width),
            ],
            1,
        ).astype(jnp.bfloat16)
        spread = jnp.einsum("gc,sgi->csi", hits, terms, preferred_element_type=jnp.float32)
        spread = spread.astype(jnp.bfloat16).reshape(row_count, -1, scenarios, block_width)
        shares = lax.all_to_all(spread, "rows", 0, 0)
        total = jnp.sum(shares.astype(jnp.float32), 0)
        adjoint = jnp.swapaxes(total, 0, 1).reshape(scenarios, local_rows)
        if position > 0:
            adjoint = (
                adjoint
                + panels[position].astype(jnp.float32)
                - targets[position - 1].astype(jnp.float32)
            )
    grad_shooting = (adjoint + defect_weight * prev_defect)[None]
    grad_controls = lax.psum(jnp.stack(input_grads, 1), "rows") * lifted_total ** (-0.5)
    grad_scale = (scenarios * horizon_steps * group_count) ** (-0.5)
    all_mu = jnp.concatenate(mu_list, 0)
    all_picked = jnp.concatenate(picked_list, 0)
    drift_sum = jnp.einsum("sno,snki->nkoi", all_mu, all_picked, preferred_element_type=jnp.float32)
    all_weighted = jnp.concatenate(weighted_list, 0)
    all_control_picked = jnp.concatenate(control_picked_list, 0)
    control_sum = jnp.einsum(
        "sjno,sjni->jnoi", all_weighted, all_control_picked, preferred_element_type=jnp.float32
    )
    drift_flat = drift_sum.reshape(drift_sum.shape[0], -1)
    grad_drift = lax.psum_scatter(drift_flat, "tm", scatter_dimension=1, tiled=True) * grad_scale
    control_flat = control_sum.reshape(control_sum.shape[0], control_sum.shape[1], -1)
    grad_control_ops = (
        lax.psum_scatter(control_flat, "tm", scatter_dimension=2, tiled=True) * grad_scale
    )
    return (grad_shooting, grad_controls, grad_drift, grad_control_ops)


MESH = pl.DeviceIdType.MESH
F32, BF16 = jnp.float32, jnp.bfloat16


NT = (((1,), (1,)), ((), ()))


def sweep_kernel(
    dcol, ccol, dvec, cvec, drift, control, ctl, start, tgt,
    gshoot, gctl, gdrift, gcontrol,
    z0, z1, z2, z3, z4, zfar, muall, terms, spread, outbox, inbox,
    lam, last, nxt, before, wts, hits, igt, igin, wsend, wfar, wall, pick,
    own_d, own_c, xd_out, xd_in, xc_out, xc_in,
    ag_s, ag_r, zl_s, zl_r, fw_s, fw_r, mu_s, mu_r, rs_s, rs_r,
    ig_s, ig_r, wx_s, wx_r, nb_s, nb_r, xd_s, xd_r, xc_s, xc_r,
):
    zs = (z0, z1, z2, z3, z4)
    steps, blocks, scen, width = muall.shape[0], *zfar.shape[2:]
    pairs = muall.shape[1]
    rows = start.shape[0]
    slots, nu = drift.shape[1], control.shape[0]
    count = rows * (slots + nu)
    tm, r = lax.axis_index("tm"), lax.axis_index("rows")
    q, x = tm // 2, tm % 2
    peers = range(1, 4)
    chunks = 4
    span = width // slots
    half = width // 2

    def row_peer(d):
        return {"tm": tm, "rows": r ^ d}

    def line_peer(e):
        return {"tm": 2 * (q ^ e) + x, "rows": r}

    barrier = pltpu.get_barrier_semaphore()
    for d in peers:
        pl.semaphore_signal(barrier, inc=1, device_id=row_peer(d), device_id_type=MESH)
        pl.semaphore_signal(barrier, inc=1, device_id=line_peer(d), device_id_type=MESH)
    group_count = lax.axis_size("tm")
    side = {"tm": tm ^ 1, "rows": r}
    after = {"tm": lax.rem(tm + 1, group_count), "rows": r}
    ahead = {"tm": lax.rem(tm + group_count - 1, group_count), "rows": r}
    for device in (side, after, ahead):
        pl.semaphore_signal(barrier, inc=1, device_id=device, device_id_type=MESH)

    zs[0][pl.ds(r * rows, rows)] = start[...]
    eye = lax.broadcasted_iota(jnp.int32, (scen, scen), 0) == lax.broadcasted_iota(
        jnp.int32, (scen, scen), 1
    )
    lane = lax.broadcasted_iota(jnp.int32, (scen, width), 1)
    for k in range(steps):
        mixed = jnp.zeros((scen, width), F32)
        for j in range(nu):
            line = jnp.broadcast_to(ctl[k, j : j + 1, :], (scen, scen))
            column = jnp.sum(jnp.where(eye, line, 0.0), axis=1, keepdims=True)
            full = jnp.broadcast_to(column, (scen, width))
            wts[k, j] = full
            mixed = jnp.where(lane // span == j, full, mixed)
        wsend[k] = mixed
    pl.semaphore_wait(barrier, 9)
    pending = []

    def send(src, dst, s, t, to, keep=True):
        copy = pltpu.make_async_remote_copy(
            src_ref=src, dst_ref=dst, send_sem=s, recv_sem=t, device_id=to, device_id_type=MESH
        )
        copy.start()
        if keep:
            pending.append(copy)
        return copy

    def panel(k, row):
        return zs[k].at[pl.ds(row * rows, rows)]

    def far(k, e, row):
        return zfar.at[k, e - 1, pl.ds(row * rows, rows)]

    def gather_whole(k, d):
        copy = pltpu.make_async_remote_copy(
            src_ref=panel(k, r), dst_ref=panel(k, r), send_sem=ag_s.at[k, d - 1],
            recv_sem=ag_r.at[k, d - 1], device_id=row_peer(d), device_id_type=MESH,
        )
        return copy

    def gather_part(k, at, size):
        for d in (2, 3, 1):
            part = zs[k].at[pl.ds(r * rows + at, size)]
            send(part, part, ag_s.at[k, d - 1], ag_r.at[k, d - 1], row_peer(d), False)

    def line_start(k):
        for e in peers:
            for h in range(2):
                send(
                    panel(k, r ^ (2 * h)), far(k, e, r ^ (2 * h)),
                    zl_s.at[k, e - 1, h], zl_r.at[k, e - 1, h], line_peer(e),
                )

    def landed_line(k, e, h):
        there = far(k, e, r ^ (2 * h))
        return pltpu.make_async_remote_copy(
            src_ref=there, dst_ref=there, send_sem=zl_s.at[k, e - 1, h],
            recv_sem=zl_r.at[k, e - 1, h], device_id=line_peer(e), device_id_type=MESH,
        )

    def pass_on(k):
        for e in peers:
            for h in range(2):
                landed_line(k, e, h).wait_recv()
                there = far(k, e, r ^ (2 * h))
                send(there, there, fw_s.at[k, e - 1, h], fw_r.at[k, e - 1, h], row_peer(1))

    gather_part(0, 0, rows)
    from_next = send(start, nxt, nb_s.at[0], nb_r.at[0], ahead)
    controls_in = [
        send(wsend, wfar.at[e - 1], wx_s.at[e - 1], wx_r.at[e - 1], line_peer(e)) for e in peers
    ]

    owner = jnp.concatenate(
        [dvec[m : m + 1, :] for m in range(slots)] + [cvec[j : j + 1, :] for j in range(nu)], 1
    )
    hits[...] = jnp.where(
        lax.broadcasted_iota(jnp.int32, (blocks, count), 0) == owner, 1.0, 0.0
    ).astype(BF16)
    prow = lax.broadcasted_iota(jnp.int32, (2 * width, width), 0)
    pcol = lax.broadcasted_iota(jnp.int32, (2 * width, width), 1)
    from_drift = lax.rem(prow + x * half, width)
    from_control = span * q + lax.rem(lax.rem(prow, span) + x * (span // 2), span)
    pick[...] = jnp.where(
        pcol == jnp.where(prow < width, from_drift, from_control), 1.0, 0.0
    ).astype(BF16)

    for k in range(steps):
        for d in peers:
            gather_whole(k, d).wait_recv()
        line_start(k)

        def forward(i, carry):
            left = [zs[k][dcol[m, i]] for m in range(slots)]
            right = [drift[i, m] for m in range(slots)]
            for j in range(nu):
                left.append((wts[k, j] * zs[k][ccol[j, i]].astype(F32)).astype(BF16))
                right.append(control[j, i])
            moved = lax.dot_general(
                jnp.concatenate(left, 1), jnp.concatenate(right, 1), NT,
                preferred_element_type=F32,
            ).astype(BF16)
            if k + 1 < steps:
                zs[k + 1][r * rows + i] = moved
            else:
                last[i] = moved
            return carry

        size = rows // chunks
        for g in range(chunks):
            lax.fori_loop(g * size, (g + 1) * size, forward, 0, unroll=True)
            if k + 1 < steps:
                gather_part(k + 1, g * size, size)
    from_prev = send(last, before, nb_s.at[1], nb_r.at[1], after)
    from_next.wait_recv()
    ends = last[...].astype(F32)
    factor = jnp.where(tm < group_count - 1, defect_weight, 0.0)
    lam[...] = ends - tgt[steps - 1].astype(F32) - factor * (nxt[...].astype(F32) - ends)
    igt[...] = jnp.zeros((scen, width), F32)
    for k in reversed(range(steps)):
        muall[k, 0] = lam[...].astype(BF16)
        for e in peers:
            send(muall.at[k, 0], muall.at[k, e], mu_s.at[k, e - 1], mu_r.at[k, e - 1], line_peer(e))

        def backward(i, carry):
            right = [drift[i, m] for m in range(slots)] + [control[j, i] for j in range(nu)]
            back = jnp.dot(
                muall[k, 0, i], jnp.concatenate(right, 1), preferred_element_type=F32
            )
            for m in range(slots):
                terms[pl.ds(m * rows + i, scen, stride=count), :] = back[
                    :, m * width : (m + 1) * width
                ]
            sums = []
            for j in range(nu):
                at = (slots + j) * width
                term = back[:, at : at + width]
                sums.append(carry[j] + term * zs[k][ccol[j, i]].astype(F32))
                terms[pl.ds((slots + j) * rows + i, scen, stride=count), :] = wts[k, j] * term
            return tuple(sums)

        zero = jnp.zeros((scen, width), F32)
        sums = lax.fori_loop(0, rows, backward, (zero,) * nu, unroll=16)
        for s in range(scen):
            spread[pl.ds(s, blocks, stride=scen), :] = jnp.dot(
                hits[...], terms[pl.ds(s * count, count), :].astype(BF16),
                preferred_element_type=F32,
            )

        def share(row):
            at = pl.multiple_of(row * (rows * scen), rows * scen)
            return spread[pl.ds(at, rows * scen), :].reshape(rows, scen, width)

        arriving = []
        for d in (2, 3, 1):
            outbox[k, d - 1] = share(r ^ d).astype(BF16)
            arriving.append(
                send(outbox.at[k, d - 1], inbox.at[k, d - 1], rs_s.at[k, d - 1], rs_r.at[k, d - 1], row_peer(d))
            )
        for j in range(nu):
            column = jnp.sum(sums[j], axis=1, keepdims=True)
            igt[...] = jnp.where(lane == k * nu + j, column, igt[...])
        pass_on(steps - 1 - k)
        if k == 0:
            partial_in = [
                send(igt, igin.at[d - 1], ig_s.at[d - 1], ig_r.at[d - 1], row_peer(d))
                for d in peers
            ]
        for copy in arriving:
            copy.wait_recv()
        total = share(r)
        for d in peers:
            total += inbox[k, d - 1].astype(F32)
        if k > 0:
            total += zs[k][pl.ds(r * rows, rows)].astype(F32) - tgt[k - 1].astype(F32)
        lam[...] = total
    for k in range(steps):
        for e in peers:
            theirs = muall.at[k, e]
            pltpu.make_async_remote_copy(
                src_ref=theirs, dst_ref=theirs, send_sem=mu_s.at[k, e - 1],
                recv_sem=mu_r.at[k, e - 1], device_id=line_peer(e), device_id_type=MESH,
            ).wait_recv()
            for h in range(2):
                there = far(k, e, r ^ 1 ^ (2 * h))
                pltpu.make_async_remote_copy(
                    src_ref=there, dst_ref=there, send_sem=fw_s.at[k, e - 1, h],
                    recv_sem=fw_r.at[k, e - 1, h], device_id=row_peer(1), device_id_type=MESH,
                ).wait_recv()
    for copy in controls_in:
        copy.wait_recv()
    scale = (scen * steps * group_count) ** (-0.5)
    depth = steps * pairs * scen
    wide = []
    for k in range(steps):
        for e in range(pairs):
            wide.append(wsend[k] if e == 0 else wfar[e - 1, k])
    wall[...] = jnp.concatenate(wide, 0).T

    def picked(c):
        parts = []
        for k in range(steps):
            parts.append(zs[k][c])
            for e in range(pairs - 1):
                parts.append(zfar[k, e, c])
        return jnp.concatenate(parts, 0)

    def sums_of(i, carry):
        mu = jnp.concatenate([muall[k, e, i] for k in range(steps) for e in range(pairs)], 0)
        chosen = lax.dot_general(pick[...], mu, NT, preferred_element_type=F32)
        plain = chosen[:width].astype(BF16)
        weighted = (chosen[width:] * wall[...]).astype(BF16)
        block = jnp.dot(plain, picked(dcol[q, i]), preferred_element_type=F32) * scale
        own_d[i] = block[:half]
        xd_out[i] = block[half:].astype(BF16)
        for j in range(nu):
            block = (
                jnp.dot(
                    weighted[j * span : (j + 1) * span], picked(ccol[j, i]),
                    preferred_element_type=F32,
                )
                * scale
            )
            own_c[j, i] = block[: span // 2]
            xc_out[i, j] = block[span // 2 :].astype(BF16)
        return carry

    crossing = []
    per = rows // xd_s.shape[0]
    for g in range(xd_s.shape[0]):
        lax.fori_loop(g * per, (g + 1) * per, sums_of, 0, unroll=True)
        part = pl.ds(g * per, per)
        crossing.append(
            (
                send(xd_out.at[part], xd_in.at[part], xd_s.at[g], xd_r.at[g], side),
                send(xc_out.at[part], xc_in.at[part], xc_s.at[g], xc_r.at[g], side),
            )
        )
    from_prev.wait_recv()
    back = jnp.where(tm > 0, defect_weight, 0.0)
    gshoot[...] = lam[...] + back * (start[...].astype(F32) - before[...].astype(F32))
    for copy in partial_in:
        copy.wait_recv()
    grads = igt[...] + igin[0] + igin[1] + igin[2]
    grads = jnp.concatenate([grads, jnp.zeros((width - scen, width), F32)], 0).T
    grads = grads * (blocks * width) ** (-0.5)
    for k in range(steps):
        gctl[k] = grads[k * nu : (k + 1) * nu, :scen]
    tile = 8
    for g, (one, two) in enumerate(crossing):
        one.wait_recv()
        two.wait_recv()

        def whole(i, carry):
            group, within = i // tile, lax.rem(i, tile)
            gdrift[pl.ds(group * (half * tile) + within, half, stride=tile), :] = own_d[
                i
            ] + xd_in[i].astype(F32)
            deep = span // 2
            for j in range(nu):
                at = (j * (rows // tile) + group) * (deep * tile) + within
                gcontrol[pl.ds(at, deep, stride=tile), :] = own_c[j, i] + xc_in[i, j].astype(F32)
            return carry

        lax.fori_loop(g * per, (g + 1) * per, whole, 0, unroll=True)
    for copy in pending:
        copy.wait_send()
    for k in range(steps):
        for d in peers:
            gather_whole(k, d).wait_send()


def shards(
    drift_blocks, drift_cols, control_blocks, control_cols, controls, shooting_states, targets
):
    group_count, row_count = lax.axis_size("tm"), lax.axis_size("rows")
    rows, slots, width, _ = drift_blocks.shape
    nu = control_blocks.shape[0]
    steps, scen, local = targets.shape
    if not (
        group_count == 2 * slots and slots == 4 and nu == 4 and row_count == 4 and steps == 5
        and scen == 8 and width == 128 and rows == 32
    ):
        return general(
            drift_blocks, drift_cols, control_blocks, control_cols, controls, shooting_states,
            targets,
        )
    blocks = rows * row_count
    pairs = group_count // 2
    first = jnp.swapaxes(shooting_states[0].reshape(scen, rows, width), 0, 1)
    tgt = jnp.swapaxes(targets.reshape(steps, scen, rows, width), 1, 2)
    ctl = jnp.swapaxes(controls, 0, 1)
    cols = jnp.swapaxes(drift_cols, 0, 1)
    span = width // slots
    count = rows * (slots + nu)
    vmem = pl.BlockSpec(memory_space=pltpu.VMEM)
    smem = pl.BlockSpec(memory_space=pltpu.SMEM)
    dma = pltpu.SemaphoreType.DMA
    groups = 8
    panel = (rows, scen, width)
    gshoot, gctl, gdrift, gcontrol = pl.pallas_call(
        sweep_kernel,
        out_shape=(
            jax.ShapeDtypeStruct(panel, F32),
            jax.ShapeDtypeStruct((steps, nu, scen), F32),
            jax.ShapeDtypeStruct((rows * width // 2, width), F32),
            jax.ShapeDtypeStruct((nu * rows * span // 2, width), F32),
        ),
        in_specs=[smem, smem] + [vmem] * 7,
        out_specs=(vmem,) * 4,
        scratch_shapes=[
            *[pltpu.VMEM((blocks, scen, width), BF16) for _ in range(5)],
            pltpu.VMEM((steps, pairs - 1, blocks, scen, width), BF16),
            pltpu.VMEM((steps, pairs, rows, scen, width), BF16),
            pltpu.VMEM((scen * count, width), F32),
            pltpu.VMEM((blocks * scen, width), F32),
            pltpu.VMEM((steps, 3, rows, scen, width), BF16),
            pltpu.VMEM((steps, 3, rows, scen, width), BF16),
            pltpu.VMEM(panel, F32),
            pltpu.VMEM(panel, BF16),
            pltpu.VMEM(panel, BF16),
            pltpu.VMEM(panel, BF16),
            pltpu.VMEM((steps, nu, scen, width), F32),
            pltpu.VMEM((blocks, count), BF16),
            pltpu.VMEM((scen, width), F32),
            pltpu.VMEM((3, scen, width), F32),
            pltpu.VMEM((steps, scen, width), F32),
            pltpu.VMEM((3, steps, scen, width), F32),
            pltpu.VMEM((width, steps * pairs * scen), F32),
            pltpu.VMEM((2 * width, width), BF16),
            pltpu.VMEM((rows, width // 2, width), F32),
            pltpu.VMEM((nu, rows, span // 2, width), F32),
            pltpu.VMEM((rows, width // 2, width), BF16),
            pltpu.VMEM((rows, width // 2, width), BF16),
            pltpu.VMEM((rows, nu, span // 2, width), BF16),
            pltpu.VMEM((rows, nu, span // 2, width), BF16),
            dma((steps, 3)), dma((steps, 3)),
            dma((steps, 3, 2)), dma((steps, 3, 2)),
            dma((steps, 3, 2)), dma((steps, 3, 2)),
            dma((steps, 3)), dma((steps, 3)),
            dma((steps, 3)), dma((steps, 3)),
            dma((3,)), dma((3,)),
            dma((3,)), dma((3,)),
            dma((2,)), dma((2,)),
            dma((groups,)), dma((groups,)),
            dma((groups,)), dma((groups,)),
        ],
        compiler_params=pltpu.CompilerParams(
            collective_id=0, has_side_effects=True, vmem_limit_bytes=60 * 2**20
        ),
        name="sweep",
    )(cols, control_cols, cols, control_cols, drift_blocks, control_blocks, ctl, first, tgt)

    grad_shooting = jnp.swapaxes(gshoot, 0, 1).reshape(1, scen, local)
    grad_drift = gdrift.reshape(rows // 8, width // 2, 8, width)
    grad_control = gcontrol.reshape(nu, rows // 8, span // 2, 8, width)
    return (
        grad_shooting,
        jnp.swapaxes(gctl, 0, 1),
        jnp.swapaxes(grad_drift, 1, 2).reshape(rows, -1),
        jnp.swapaxes(grad_control, 2, 3).reshape(nu, rows, -1),
    )


def solution(mesh):
    return jax.shard_map(
        shards,
        mesh=mesh,
        in_specs=(
            P("rows", None, None, None),
            P("rows", None),
            P(None, "rows", None, None),
            P(None, "rows"),
            P(None, "tm", None),
            P("tm", None, "rows"),
            P("tm", None, "rows"),
        ),
        out_specs=(
            P("tm", None, "rows"),
            P(None, "tm", None),
            P("rows", "tm"),
            P(None, "rows", "tm"),
        ),
        check_vma=False,
    )
```

```python
import jax
import jax.numpy as jnp
from jax import lax
from jax.experimental import pallas as pl
from jax.experimental.pallas import tpu as pltpu
from jax.sharding import PartitionSpec as P

defect_weight = 2.0


def passed_along(value, axis, by):
    count = lax.axis_size(axis)
    pairs = [(i, i + by) for i in range(count) if 0 <= i + by < count]
    return lax.ppermute(value, axis, pairs)


def step_terms(gathered, block_width, drift_blocks, drift_cols, control_blocks, control_cols):
    blocks = gathered.reshape(gathered.shape[0], -1, block_width)
    total = jnp.arange(blocks.shape[1])
    drift_hits = (drift_cols[..., None] == total).astype(jnp.bfloat16)
    control_hits = (control_cols[..., None] == total).astype(jnp.bfloat16)
    picked = jnp.einsum(
        "nkb,sbi->snki", drift_hits, blocks, preferred_element_type=jnp.float32
    ).astype(jnp.bfloat16)
    drift_out = jnp.einsum(
        "snki,nkoi->sno", picked, drift_blocks, preferred_element_type=jnp.float32
    )
    control_picked = jnp.einsum(
        "jnb,sbi->sjni", control_hits, blocks, preferred_element_type=jnp.float32
    ).astype(jnp.bfloat16)
    control_out = jnp.einsum(
        "sjni,jnoi->sjno", control_picked, control_blocks, preferred_element_type=jnp.float32
    )
    return (picked, drift_out, control_picked, control_out)


def general(
    drift_blocks, drift_cols, control_blocks, control_cols, controls, shooting_states, targets
):
    block_width = drift_blocks.shape[-1]
    scenarios = shooting_states.shape[1]
    local_rows = shooting_states.shape[2]
    horizon_steps = targets.shape[0]
    group_count = lax.axis_size("tm")
    group_index = lax.axis_index("tm")
    total_blocks = drift_blocks.shape[0] * lax.axis_size("rows")
    lifted_total = local_rows * lax.axis_size("rows")
    operators = (drift_blocks, drift_cols, control_blocks, control_cols)
    row_count = lax.axis_size("rows")
    targets_of = jnp.concatenate([drift_cols.reshape(-1), control_cols.reshape(-1)])
    hits = (targets_of[:, None] == jnp.arange(total_blocks)[None]).astype(jnp.bfloat16)
    first_panel = shooting_states[0]
    panels = [first_panel]
    stored = []
    state_panel = first_panel
    for position in range(horizon_steps):
        gathered = lax.all_gather(state_panel, "rows", axis=1, tiled=True)
        step_parts = step_terms(gathered, block_width, *operators)
        stored.append(step_parts)
        weights = controls[:, position].T[:, :, None, None]
        mixed = step_parts[1] + jnp.sum(weights * step_parts[3], axis=1)
        state_panel = mixed.reshape(scenarios, local_rows).astype(jnp.bfloat16)
        panels.append(state_panel)
    group_end = panels[-1]
    next_start = passed_along(first_panel, "tm", -1)
    prev_end = passed_along(group_end, "tm", 1)
    end_wide = group_end.astype(jnp.float32)
    defect = jnp.where(
        group_index < group_count - 1, next_start.astype(jnp.float32) - end_wide, 0.0
    )
    prev_defect = jnp.where(
        group_index > 0, first_panel.astype(jnp.float32) - prev_end.astype(jnp.float32), 0.0
    )
    adjoint = end_wide - targets[horizon_steps - 1].astype(jnp.float32) - defect_weight * defect
    input_grads = [None] * horizon_steps
    mu_list = []
    picked_list = []
    weighted_list = []
    control_picked_list = []
    for position in reversed(range(horizon_steps)):
        adjoint_half = adjoint.astype(jnp.bfloat16)
        picked, drift_out, control_picked, control_out = stored[position]
        mu_blocks = adjoint_half.reshape(scenarios, -1, block_width)
        mu_wide = mu_blocks.astype(jnp.float32)
        weights = controls[:, position].T[:, :, None, None]
        input_grads[position] = jnp.sum(mu_wide[:, None] * control_out, axis=(2, 3)).T
        weighted = (mu_wide[:, None] * weights).astype(jnp.bfloat16)
        mu_list.append(mu_blocks)
        picked_list.append(picked)
        weighted_list.append(weighted)
        control_picked_list.append(control_picked)
        drift_back = jnp.einsum(
            "sno,nkoi->snki", mu_blocks, drift_blocks, preferred_element_type=jnp.float32
        )
        control_back = (
            jnp.einsum(
                "sno,jnoi->sjni", mu_blocks, control_blocks, preferred_element_type=jnp.float32
            )
            * weights
        )
        terms = jnp.concatenate(
            [
                drift_back.reshape(scenarios, -1, block_width),
                control_back.reshape(scenarios, -1, block_width),
            ],
            1,
        ).astype(jnp.bfloat16)
        spread = jnp.einsum("gc,sgi->csi", hits, terms, preferred_element_type=jnp.float32)
        spread = spread.astype(jnp.bfloat16).reshape(row_count, -1, scenarios, block_width)
        shares = lax.all_to_all(spread, "rows", 0, 0)
        total = jnp.sum(shares.astype(jnp.float32), 0)
        adjoint = jnp.swapaxes(total, 0, 1).reshape(scenarios, local_rows)
        if position > 0:
            adjoint = (
                adjoint
                + panels[position].astype(jnp.float32)
                - targets[position - 1].astype(jnp.float32)
            )
    grad_shooting = (adjoint + defect_weight * prev_defect)[None]
    grad_controls = lax.psum(jnp.stack(input_grads, 1), "rows") * lifted_total ** (-0.5)
    grad_scale = (scenarios * horizon_steps * group_count) ** (-0.5)
    all_mu = jnp.concatenate(mu_list, 0)
    all_picked = jnp.concatenate(picked_list, 0)
    drift_sum = jnp.einsum("sno,snki->nkoi", all_mu, all_picked, preferred_element_type=jnp.float32)
    all_weighted = jnp.concatenate(weighted_list, 0)
    all_control_picked = jnp.concatenate(control_picked_list, 0)
    control_sum = jnp.einsum(
        "sjno,sjni->jnoi", all_weighted, all_control_picked, preferred_element_type=jnp.float32
    )
    drift_flat = drift_sum.reshape(drift_sum.shape[0], -1)
    grad_drift = lax.psum_scatter(drift_flat, "tm", scatter_dimension=1, tiled=True) * grad_scale
    control_flat = control_sum.reshape(control_sum.shape[0], control_sum.shape[1], -1)
    grad_control_ops = (
        lax.psum_scatter(control_flat, "tm", scatter_dimension=2, tiled=True) * grad_scale
    )
    return (grad_shooting, grad_controls, grad_drift, grad_control_ops)


MESH = pl.DeviceIdType.MESH
F32, BF16 = jnp.float32, jnp.bfloat16


NT = (((1,), (1,)), ((), ()))


def sweep_kernel(
    dcol, ccol, dvec, cvec, drift, control, ctl, start, tgt,
    gshoot, gctl, own_d, own_c, xd_in, xc_in,
    z0, z1, z2, z3, z4, zfar, muall, terms, spread, outbox, inbox,
    lam, last, nxt, before, wts, hits, igt, igin, wsend, wfar, wall, pick,
    xd_out, xc_out,
    ag_s, ag_r, zl_s, zl_r, zq_s, zy_s, zy_r, zc_s, zc_r, mu_s, mu_r, mq_s, rs_s, rs_r,
    ig_s, ig_r, wx_s, wx_r, nb_s, nb_r, xd_s, xd_r, xc_s, xc_r,
):
    zs = (z0, z1, z2, z3, z4)
    steps, blocks, scen, width = muall.shape[0], *zfar.shape[2:]
    pairs = muall.shape[1]
    rows = start.shape[0]
    slots, nu = drift.shape[1], control.shape[0]
    count = rows * (slots + nu)
    tm, r = lax.axis_index("tm"), lax.axis_index("rows")
    q, x = tm // 2, tm % 2
    peers = range(1, 4)
    chunks = 4
    span = width // slots
    half = width // 2

    def row_peer(d):
        return {"tm": tm, "rows": r ^ d}

    def line_peer(e):
        return {"tm": 2 * (q ^ e) + x, "rows": r}

    barrier = pltpu.get_barrier_semaphore()
    for d in peers:
        pl.semaphore_signal(barrier, inc=1, device_id=row_peer(d), device_id_type=MESH)
        pl.semaphore_signal(barrier, inc=1, device_id=line_peer(d), device_id_type=MESH)
    group_count = lax.axis_size("tm")
    side = {"tm": tm ^ 1, "rows": r}
    after = {"tm": lax.rem(tm + 1, group_count), "rows": r}
    ahead = {"tm": lax.rem(tm + group_count - 1, group_count), "rows": r}
    for device in (side, after, ahead):
        pl.semaphore_signal(barrier, inc=1, device_id=device, device_id_type=MESH)

    zs[0][pl.ds(r * rows, rows)] = start[...]
    eye = lax.broadcasted_iota(jnp.int32, (scen, scen), 0) == lax.broadcasted_iota(
        jnp.int32, (scen, scen), 1
    )
    lane = lax.broadcasted_iota(jnp.int32, (scen, width), 1)
    for k in range(steps):
        mixed = jnp.zeros((scen, width), F32)
        for j in range(nu):
            line = jnp.broadcast_to(ctl[k, j : j + 1, :], (scen, scen))
            column = jnp.sum(jnp.where(eye, line, 0.0), axis=1, keepdims=True)
            full = jnp.broadcast_to(column, (scen, width))
            wts[k, j] = full
            mixed = jnp.where(lane // span == j, full, mixed)
        wsend[k] = mixed
    pl.semaphore_wait(barrier, 9)
    pending = []

    def send(src, dst, s, t, to, keep=True):
        copy = pltpu.make_async_remote_copy(
            src_ref=src, dst_ref=dst, send_sem=s, recv_sem=t, device_id=to, device_id_type=MESH
        )
        copy.start()
        if keep:
            pending.append(copy)
        return copy

    def panel(k, row):
        return zs[k].at[pl.ds(row * rows, rows)]

    def far(k, e, row):
        return zfar.at[k, e - 1, pl.ds(row * rows, rows)]

    def gather_whole(k, d):
        copy = pltpu.make_async_remote_copy(
            src_ref=panel(k, r), dst_ref=panel(k, r), send_sem=ag_s.at[k, d - 1],
            recv_sem=ag_r.at[k, d - 1], device_id=row_peer(d), device_id_type=MESH,
        )
        return copy

    def gather_part(k, at, size):
        for d in (2, 3, 1):
            part = zs[k].at[pl.ds(r * rows + at, size)]
            send(part, part, ag_s.at[k, d - 1], ag_r.at[k, d - 1], row_peer(d), False)

    inner = jnp.logical_or(q == 1, q == 2)
    outer = jnp.logical_not(inner)

    def far_copy(k, e, row, s, t, to):
        there = far(k, e, row)
        return pltpu.make_async_remote_copy(
            src_ref=there, dst_ref=there, send_sem=s, recv_sem=t, device_id=to,
            device_id_type=MESH,
        )

    def line_copy(k, e):
        return pltpu.make_async_remote_copy(
            src_ref=panel(k, r), dst_ref=far(k, e, r), send_sem=zl_s.at[k, e - 1],
            recv_sem=zl_r.at[k, e - 1], device_id=line_peer(e), device_id_type=MESH,
        )

    def line_on(k):
        return pltpu.make_async_remote_copy(
            src_ref=far(k, 2, r), dst_ref=far(k, 3, r), send_sem=zq_s.at[k],
            recv_sem=zl_r.at[k, 2], device_id=line_peer(1), device_id_type=MESH,
        )

    def over_y(k, e):
        return far_copy(k, e, r, zy_s.at[k, e - 1], zy_r.at[k, e - 1], row_peer(2))

    def over_core(k, e, h):
        return far_copy(k, e, r ^ (2 * h), zc_s.at[k, e - 1, h], zc_r.at[k, e - 1, h], row_peer(1))

    def mu_copy(k, e):
        return pltpu.make_async_remote_copy(
            src_ref=muall.at[k, 0], dst_ref=muall.at[k, e], send_sem=mu_s.at[k, e - 1],
            recv_sem=mu_r.at[k, e - 1], device_id=line_peer(e), device_id_type=MESH,
        )

    def mu_on(k):
        return pltpu.make_async_remote_copy(
            src_ref=muall.at[k, 2], dst_ref=muall.at[k, 3], send_sem=mq_s.at[k],
            recv_sem=mu_r.at[k, 2], device_id=line_peer(1), device_id_type=MESH,
        )

    def move_states(t):
        if t < steps:
            line_copy(t, 1).start()
            line_copy(t, 2).start()
            pl.when(inner)(line_copy(t, 3).start)
        k = t - 2
        if 0 <= k < steps:
            for e in (1, 2):
                line_copy(k, e).wait_recv()
                over_y(k, e).start()
                over_core(k, e, 0).start()
            pl.when(inner)(line_on(k).start)
        k = t - 3
        if 0 <= k < steps:
            line_copy(k, 3).wait_recv()
            over_y(k, 3).start()
            over_core(k, 3, 0).start()
            for e in (1, 2):
                over_y(k, e).wait_recv()
                over_core(k, e, 1).start()
        k = t - 4
        if 0 <= k < steps:
            over_y(k, 3).wait_recv()
            over_core(k, 3, 1).start()

    gather_part(0, 0, rows)
    from_next = send(start, nxt, nb_s.at[0], nb_r.at[0], ahead)
    controls_in = [
        send(wsend, wfar.at[e - 1], wx_s.at[e - 1], wx_r.at[e - 1], line_peer(e)) for e in peers
    ]

    owner = jnp.concatenate(
        [dvec[m : m + 1, :] for m in range(slots)] + [cvec[j : j + 1, :] for j in range(nu)], 1
    )
    hits[...] = jnp.where(
        lax.broadcasted_iota(jnp.int32, (blocks, count), 0) == owner, 1.0, 0.0
    ).astype(BF16)
    prow = lax.broadcasted_iota(jnp.int32, (2 * width, width), 0)
    pcol = lax.broadcasted_iota(jnp.int32, (2 * width, width), 1)
    from_drift = lax.rem(prow + x * half, width)
    from_control = span * q + lax.rem(lax.rem(prow, span) + x * (span // 2), span)
    pick[...] = jnp.where(
        pcol == jnp.where(prow < width, from_drift, from_control), 1.0, 0.0
    ).astype(BF16)

    for k in range(steps):
        for d in peers:
            gather_whole(k, d).wait_recv()
        move_states(k)

        def forward(i, carry):
            left = [zs[k][dcol[m, i]] for m in range(slots)]
            right = [drift[i, m] for m in range(slots)]
            for j in range(nu):
                left.append((wts[k, j] * zs[k][ccol[j, i]].astype(F32)).astype(BF16))
                right.append(control[j, i])
            moved = lax.dot_general(
                jnp.concatenate(left, 1), jnp.concatenate(right, 1), NT,
                preferred_element_type=F32,
            ).astype(BF16)
            if k + 1 < steps:
                zs[k + 1][r * rows + i] = moved
            else:
                last[i] = moved
            return carry

        size = rows // chunks
        for g in range(chunks):
            lax.fori_loop(g * size, (g + 1) * size, forward, 0, unroll=True)
            if k + 1 < steps:
                gather_part(k + 1, g * size, size)
    from_prev = send(last, before, nb_s.at[1], nb_r.at[1], after)
    from_next.wait_recv()
    ends = last[...].astype(F32)
    factor = jnp.where(tm < group_count - 1, defect_weight, 0.0)
    lam[...] = ends - tgt[steps - 1].astype(F32) - factor * (nxt[...].astype(F32) - ends)
    igt[...] = jnp.zeros((scen, width), F32)
    for k in reversed(range(steps)):
        muall[k, 0] = lam[...].astype(BF16)
        mu_copy(k, 1).start()
        mu_copy(k, 2).start()
        if k > 0:
            pl.when(inner)(mu_copy(k, 3).start)
        else:
            mu_copy(k, 3).start()

        def backward(i, carry):
            right = [drift[i, m] for m in range(slots)] + [control[j, i] for j in range(nu)]
            back = jnp.dot(
                muall[k, 0, i], jnp.concatenate(right, 1), preferred_element_type=F32
            )
            for m in range(slots):
                terms[pl.ds(m * rows + i, scen, stride=count), :] = back[
                    :, m * width : (m + 1) * width
                ]
            sums = []
            for j in range(nu):
                at = (slots + j) * width
                term = back[:, at : at + width]
                sums.append(carry[j] + term * zs[k][ccol[j, i]].astype(F32))
                terms[pl.ds((slots + j) * rows + i, scen, stride=count), :] = wts[k, j] * term
            return tuple(sums)

        zero = jnp.zeros((scen, width), F32)
        sums = lax.fori_loop(0, rows, backward, (zero,) * nu, unroll=16)
        for s in range(scen):
            spread[pl.ds(s, blocks, stride=scen), :] = jnp.dot(
                hits[...], terms[pl.ds(s * count, count), :].astype(BF16),
                preferred_element_type=F32,
            )

        def share(row):
            at = pl.multiple_of(row * (rows * scen), rows * scen)
            return spread[pl.ds(at, rows * scen), :].reshape(rows, scen, width)

        arriving = []
        for d in (2, 3, 1):
            outbox[k, d - 1] = share(r ^ d).astype(BF16)
            arriving.append(
                send(outbox.at[k, d - 1], inbox.at[k, d - 1], rs_s.at[k, d - 1], rs_r.at[k, d - 1], row_peer(d))
            )
        for j in range(nu):
            column = jnp.sum(sums[j], axis=1, keepdims=True)
            igt[...] = jnp.where(lane == k * nu + j, column, igt[...])
        move_states(2 * steps - 1 - k)
        if k + 1 < steps:
            mu_copy(k + 1, 2).wait_recv()
            pl.when(inner)(mu_on(k + 1).start)
        if k == 0:
            partial_in = [
                send(igt, igin.at[d - 1], ig_s.at[d - 1], ig_r.at[d - 1], row_peer(d))
                for d in peers
            ]
        for copy in arriving:
            copy.wait_recv()
        total = share(r)
        for d in peers:
            total += inbox[k, d - 1].astype(F32)
        if k > 0:
            total += zs[k][pl.ds(r * rows, rows)].astype(F32) - tgt[k - 1].astype(F32)
        lam[...] = total
    for k in range(steps):
        for e in peers:
            if e != 2 or k == 0:
                mu_copy(k, e).wait_recv()
            for h in range(2):
                over_core(k, e, h).wait_recv()
    for copy in controls_in:
        copy.wait_recv()
    scale = (scen * steps * group_count) ** (-0.5)
    depth = steps * pairs * scen
    wide = []
    for k in range(steps):
        for e in range(pairs):
            wide.append(wsend[k] if e == 0 else wfar[e - 1, k])
    wall[...] = jnp.concatenate(wide, 0).T

    def picked(c):
        parts = []
        for k in range(steps):
            parts.append(zs[k][c])
            for e in range(pairs - 1):
                parts.append(zfar[k, e, c])
        return jnp.concatenate(parts, 0)

    def sums_of(i, carry):
        mu = jnp.concatenate([muall[k, e, i] for k in range(steps) for e in range(pairs)], 0)
        chosen = lax.dot_general(pick[...], mu, NT, preferred_element_type=F32)
        plain = chosen[:width].astype(BF16)
        weighted = (chosen[width:] * wall[...]).astype(BF16)
        block = jnp.dot(plain, picked(dcol[q, i]), preferred_element_type=F32) * scale
        own_d[i] = block[:half]
        xd_out[i] = block[half:].astype(BF16)
        for j in range(nu):
            block = (
                jnp.dot(
                    weighted[j * span : (j + 1) * span], picked(ccol[j, i]),
                    preferred_element_type=F32,
                )
                * scale
            )
            own_c[j, i] = block[: span // 2]
            xc_out[i, j] = block[span // 2 :].astype(BF16)
        return carry

    crossing = []
    per = rows // xd_s.shape[0]
    for g in range(xd_s.shape[0]):
        lax.fori_loop(g * per, (g + 1) * per, sums_of, 0, unroll=True)
        part = pl.ds(g * per, per)
        crossing.append(
            (
                send(xd_out.at[part], xd_in.at[part], xd_s.at[g], xd_r.at[g], side),
                send(xc_out.at[part], xc_in.at[part], xc_s.at[g], xc_r.at[g], side),
            )
        )
    from_prev.wait_recv()
    back = jnp.where(tm > 0, defect_weight, 0.0)
    gshoot[...] = lam[...] + back * (start[...].astype(F32) - before[...].astype(F32))
    for copy in partial_in:
        copy.wait_recv()
    grads = igt[...] + igin[0] + igin[1] + igin[2]
    grads = jnp.concatenate([grads, jnp.zeros((width - scen, width), F32)], 0).T
    grads = grads * (blocks * width) ** (-0.5)
    for k in range(steps):
        gctl[k] = grads[k * nu : (k + 1) * nu, :scen]
    for one, two in crossing:
        one.wait_recv()
        two.wait_recv()
    for copy in pending:
        copy.wait_send()
    for k in range(steps):
        for d in peers:
            gather_whole(k, d).wait_send()
        for e in (1, 2):
            line_copy(k, e).wait_send()
            mu_copy(k, e).wait_send()
        pl.when(inner)(line_copy(k, 3).wait_send)
        pl.when(inner)(line_on(k).wait_send)
        for e in peers:
            over_y(k, e).wait_send()
            for h in range(2):
                over_core(k, e, h).wait_send()
        if k > 0:
            pl.when(inner)(mu_copy(k, 3).wait_send)
            pl.when(inner)(mu_on(k).wait_send)
        else:
            mu_copy(k, 3).wait_send()


def finish_kernel(own_d, xd_in, own_c, xc_in, shoot_in, ctl_in, gdrift, gcontrol, gshoot, gctl):
    rows, half, _ = own_d.shape
    nu, deep, tile = xc_in.shape[1], xc_in.shape[2], 8

    def whole(i, carry):
        group, within = i // tile, lax.rem(i, tile)
        gdrift[pl.ds(group * (half * tile) + within, half, stride=tile), :] = own_d[i] + xd_in[
            i
        ].astype(F32)
        for j in range(nu):
            at = (j * (rows // tile) + group) * (deep * tile) + within
            gcontrol[pl.ds(at, deep, stride=tile), :] = own_c[j, i] + xc_in[i, j].astype(F32)
        return carry

    lax.fori_loop(0, rows, whole, 0, unroll=8)
    gshoot[...] = shoot_in[...]
    gctl[...] = ctl_in[...]


def shards(
    drift_blocks, drift_cols, control_blocks, control_cols, controls, shooting_states, targets
):
    group_count, row_count = lax.axis_size("tm"), lax.axis_size("rows")
    rows, slots, width, _ = drift_blocks.shape
    nu = control_blocks.shape[0]
    steps, scen, local = targets.shape
    if not (
        group_count == 2 * slots and slots == 4 and nu == 4 and row_count == 4 and steps == 5
        and scen == 8 and width == 128 and rows == 32
    ):
        return general(
            drift_blocks, drift_cols, control_blocks, control_cols, controls, shooting_states,
            targets,
        )
    blocks = rows * row_count
    pairs = group_count // 2
    first = jnp.swapaxes(shooting_states[0].reshape(scen, rows, width), 0, 1)
    tgt = jnp.swapaxes(targets.reshape(steps, scen, rows, width), 1, 2)
    ctl = jnp.swapaxes(controls, 0, 1)
    cols = jnp.swapaxes(drift_cols, 0, 1)
    span = width // slots
    count = rows * (slots + nu)
    vmem = pl.BlockSpec(memory_space=pltpu.VMEM)
    smem = pl.BlockSpec(memory_space=pltpu.SMEM)
    dma = pltpu.SemaphoreType.DMA
    groups = 8
    panel = (rows, scen, width)
    gshoot, gctl, own_d, own_c, xd_in, xc_in = pl.pallas_call(
        sweep_kernel,
        out_shape=(
            jax.ShapeDtypeStruct(panel, F32),
            jax.ShapeDtypeStruct((steps, nu, scen), F32),
            jax.ShapeDtypeStruct((rows, width // 2, width), F32),
            jax.ShapeDtypeStruct((nu, rows, span // 2, width), F32),
            jax.ShapeDtypeStruct((rows, width // 2, width), BF16),
            jax.ShapeDtypeStruct((rows, nu, span // 2, width), BF16),
        ),
        in_specs=[smem, smem] + [vmem] * 7,
        out_specs=(vmem,) * 6,
        scratch_shapes=[
            *[pltpu.VMEM((blocks, scen, width), BF16) for _ in range(5)],
            pltpu.VMEM((steps, pairs - 1, blocks, scen, width), BF16),
            pltpu.VMEM((steps, pairs, rows, scen, width), BF16),
            pltpu.VMEM((scen * count, width), F32),
            pltpu.VMEM((blocks * scen, width), F32),
            pltpu.VMEM((steps, 3, rows, scen, width), BF16),
            pltpu.VMEM((steps, 3, rows, scen, width), BF16),
            pltpu.VMEM(panel, F32),
            pltpu.VMEM(panel, BF16),
            pltpu.VMEM(panel, BF16),
            pltpu.VMEM(panel, BF16),
            pltpu.VMEM((steps, nu, scen, width), F32),
            pltpu.VMEM((blocks, count), BF16),
            pltpu.VMEM((scen, width), F32),
            pltpu.VMEM((3, scen, width), F32),
            pltpu.VMEM((steps, scen, width), F32),
            pltpu.VMEM((3, steps, scen, width), F32),
            pltpu.VMEM((width, steps * pairs * scen), F32),
            pltpu.VMEM((2 * width, width), BF16),
            pltpu.VMEM((rows, width // 2, width), BF16),
            pltpu.VMEM((rows, nu, span // 2, width), BF16),
            dma((steps, 3)), dma((steps, 3)),
            dma((steps, 3)), dma((steps, 3)), dma((steps,)),
            dma((steps, 3)), dma((steps, 3)),
            dma((steps, 3, 2)), dma((steps, 3, 2)),
            dma((steps, 3)), dma((steps, 3)), dma((steps,)),
            dma((steps, 3)), dma((steps, 3)),
            dma((3,)), dma((3,)),
            dma((3,)), dma((3,)),
            dma((2,)), dma((2,)),
            dma((groups,)), dma((groups,)),
            dma((groups,)), dma((groups,)),
        ],
        compiler_params=pltpu.CompilerParams(
            collective_id=0, has_side_effects=True, vmem_limit_bytes=60 * 2**20
        ),
        name="sweep",
    )(cols, control_cols, cols, control_cols, drift_blocks, control_blocks, ctl, first, tgt)

    gdrift, gcontrol, gshoot, gctl = pl.pallas_call(
        finish_kernel,
        out_shape=(
            jax.ShapeDtypeStruct((rows * width // 2, width), F32),
            jax.ShapeDtypeStruct((nu * rows * span // 2, width), F32),
            jax.ShapeDtypeStruct(panel, F32),
            jax.ShapeDtypeStruct((steps, nu, scen), F32),
        ),
        in_specs=[vmem] * 6,
        out_specs=(vmem,) * 4,
        name="finish",
    )(own_d, xd_in, own_c, xc_in, gshoot, gctl)

    grad_shooting = jnp.swapaxes(gshoot, 0, 1).reshape(1, scen, local)
    grad_drift = gdrift.reshape(rows // 8, width // 2, 8, width)
    grad_control = gcontrol.reshape(nu, rows // 8, span // 2, 8, width)
    return (
        grad_shooting,
        jnp.swapaxes(gctl, 0, 1),
        jnp.swapaxes(grad_drift, 1, 2).reshape(rows, -1),
        jnp.swapaxes(grad_control, 2, 3).reshape(nu, rows, -1),
    )


def solution(mesh):
    return jax.shard_map(
        shards,
        mesh=mesh,
        in_specs=(
            P("rows", None, None, None),
            P("rows", None),
            P(None, "rows", None, None),
            P(None, "rows"),
            P(None, "tm", None),
            P("tm", None, "rows"),
            P("tm", None, "rows"),
        ),
        out_specs=(
            P("tm", None, "rows"),
            P(None, "tm", None),
            P("rows", "tm"),
            P(None, "rows", "tm"),
        ),
        check_vma=False,
    )
```

```python
import jax
import jax.numpy as jnp
from jax import lax
from jax.experimental import pallas as pl
from jax.experimental.pallas import tpu as pltpu
from jax.sharding import PartitionSpec as P

defect_weight = 2.0


def passed_along(value, axis, by):
    count = lax.axis_size(axis)
    pairs = [(i, i + by) for i in range(count) if 0 <= i + by < count]
    return lax.ppermute(value, axis, pairs)


def step_terms(gathered, block_width, drift_blocks, drift_cols, control_blocks, control_cols):
    blocks = gathered.reshape(gathered.shape[0], -1, block_width)
    total = jnp.arange(blocks.shape[1])
    drift_hits = (drift_cols[..., None] == total).astype(jnp.bfloat16)
    control_hits = (control_cols[..., None] == total).astype(jnp.bfloat16)
    picked = jnp.einsum(
        "nkb,sbi->snki", drift_hits, blocks, preferred_element_type=jnp.float32
    ).astype(jnp.bfloat16)
    drift_out = jnp.einsum(
        "snki,nkoi->sno", picked, drift_blocks, preferred_element_type=jnp.float32
    )
    control_picked = jnp.einsum(
        "jnb,sbi->sjni", control_hits, blocks, preferred_element_type=jnp.float32
    ).astype(jnp.bfloat16)
    control_out = jnp.einsum(
        "sjni,jnoi->sjno", control_picked, control_blocks, preferred_element_type=jnp.float32
    )
    return (picked, drift_out, control_picked, control_out)


def general(
    drift_blocks, drift_cols, control_blocks, control_cols, controls, shooting_states, targets
):
    block_width = drift_blocks.shape[-1]
    scenarios = shooting_states.shape[1]
    local_rows = shooting_states.shape[2]
    horizon_steps = targets.shape[0]
    group_count = lax.axis_size("tm")
    group_index = lax.axis_index("tm")
    total_blocks = drift_blocks.shape[0] * lax.axis_size("rows")
    lifted_total = local_rows * lax.axis_size("rows")
    operators = (drift_blocks, drift_cols, control_blocks, control_cols)
    row_count = lax.axis_size("rows")
    targets_of = jnp.concatenate([drift_cols.reshape(-1), control_cols.reshape(-1)])
    hits = (targets_of[:, None] == jnp.arange(total_blocks)[None]).astype(jnp.bfloat16)
    first_panel = shooting_states[0]
    panels = [first_panel]
    stored = []
    state_panel = first_panel
    for position in range(horizon_steps):
        gathered = lax.all_gather(state_panel, "rows", axis=1, tiled=True)
        step_parts = step_terms(gathered, block_width, *operators)
        stored.append(step_parts)
        weights = controls[:, position].T[:, :, None, None]
        mixed = step_parts[1] + jnp.sum(weights * step_parts[3], axis=1)
        state_panel = mixed.reshape(scenarios, local_rows).astype(jnp.bfloat16)
        panels.append(state_panel)
    group_end = panels[-1]
    next_start = passed_along(first_panel, "tm", -1)
    prev_end = passed_along(group_end, "tm", 1)
    end_wide = group_end.astype(jnp.float32)
    defect = jnp.where(
        group_index < group_count - 1, next_start.astype(jnp.float32) - end_wide, 0.0
    )
    prev_defect = jnp.where(
        group_index > 0, first_panel.astype(jnp.float32) - prev_end.astype(jnp.float32), 0.0
    )
    adjoint = end_wide - targets[horizon_steps - 1].astype(jnp.float32) - defect_weight * defect
    input_grads = [None] * horizon_steps
    mu_list = []
    picked_list = []
    weighted_list = []
    control_picked_list = []
    for position in reversed(range(horizon_steps)):
        adjoint_half = adjoint.astype(jnp.bfloat16)
        picked, drift_out, control_picked, control_out = stored[position]
        mu_blocks = adjoint_half.reshape(scenarios, -1, block_width)
        mu_wide = mu_blocks.astype(jnp.float32)
        weights = controls[:, position].T[:, :, None, None]
        input_grads[position] = jnp.sum(mu_wide[:, None] * control_out, axis=(2, 3)).T
        weighted = (mu_wide[:, None] * weights).astype(jnp.bfloat16)
        mu_list.append(mu_blocks)
        picked_list.append(picked)
        weighted_list.append(weighted)
        control_picked_list.append(control_picked)
        drift_back = jnp.einsum(
            "sno,nkoi->snki", mu_blocks, drift_blocks, preferred_element_type=jnp.float32
        )
        control_back = (
            jnp.einsum(
                "sno,jnoi->sjni", mu_blocks, control_blocks, preferred_element_type=jnp.float32
            )
            * weights
        )
        terms = jnp.concatenate(
            [
                drift_back.reshape(scenarios, -1, block_width),
                control_back.reshape(scenarios, -1, block_width),
            ],
            1,
        ).astype(jnp.bfloat16)
        spread = jnp.einsum("gc,sgi->csi", hits, terms, preferred_element_type=jnp.float32)
        spread = spread.astype(jnp.bfloat16).reshape(row_count, -1, scenarios, block_width)
        shares = lax.all_to_all(spread, "rows", 0, 0)
        total = jnp.sum(shares.astype(jnp.float32), 0)
        adjoint = jnp.swapaxes(total, 0, 1).reshape(scenarios, local_rows)
        if position > 0:
            adjoint = (
                adjoint
                + panels[position].astype(jnp.float32)
                - targets[position - 1].astype(jnp.float32)
            )
    grad_shooting = (adjoint + defect_weight * prev_defect)[None]
    grad_controls = lax.psum(jnp.stack(input_grads, 1), "rows") * lifted_total ** (-0.5)
    grad_scale = (scenarios * horizon_steps * group_count) ** (-0.5)
    all_mu = jnp.concatenate(mu_list, 0)
    all_picked = jnp.concatenate(picked_list, 0)
    drift_sum = jnp.einsum("sno,snki->nkoi", all_mu, all_picked, preferred_element_type=jnp.float32)
    all_weighted = jnp.concatenate(weighted_list, 0)
    all_control_picked = jnp.concatenate(control_picked_list, 0)
    control_sum = jnp.einsum(
        "sjno,sjni->jnoi", all_weighted, all_control_picked, preferred_element_type=jnp.float32
    )
    drift_flat = drift_sum.reshape(drift_sum.shape[0], -1)
    grad_drift = lax.psum_scatter(drift_flat, "tm", scatter_dimension=1, tiled=True) * grad_scale
    control_flat = control_sum.reshape(control_sum.shape[0], control_sum.shape[1], -1)
    grad_control_ops = (
        lax.psum_scatter(control_flat, "tm", scatter_dimension=2, tiled=True) * grad_scale
    )
    return (grad_shooting, grad_controls, grad_drift, grad_control_ops)


MESH = pl.DeviceIdType.MESH
F32, BF16 = jnp.float32, jnp.bfloat16


NT = (((1,), (1,)), ((), ()))


def sweep_kernel(
    dcol, ccol, dvec, cvec, drift_far, control_far, ctl, start, tgt,
    gshoot, gctl, own_d, own_c, xd_in, xc_in,
    z0, z1, z2, z3, z4, zfar, muall, terms, spread, outbox, inbox,
    lam, last, nxt, before, wts, hits, igt, igin, wsend, wfar, wall, pick,
    xd_out, xc_out, drift, control, turned,
    dr_s, co_s, ag_s, ag_r, ay_s, ay_r, af_s, zl_s, zl_r, zq_s, zy_s, zy_r, zc_s, zc_r, mu_s, mu_r, mq_s, m0_s, m0_r, rs_s, rs_r,
    ig_s, ig_r, wx_s, wx_r, nb_s, nb_r, xd_s, xd_r, xc_s, xc_r,
):
    zs = (z0, z1, z2, z3, z4)
    steps, blocks, scen, width = muall.shape[0], *zfar.shape[2:]
    pairs = muall.shape[1]
    rows = start.shape[0]
    slots, nu = drift.shape[1], control.shape[0]
    count = rows * (slots + nu)
    tm, r = lax.axis_index("tm"), lax.axis_index("rows")
    q, x = tm // 2, tm % 2
    peers = range(1, 4)
    chunks = 4
    span = width // slots
    half = width // 2

    def row_peer(d):
        return {"tm": tm, "rows": r ^ d}

    def line_peer(e):
        return {"tm": 2 * (q ^ e) + x, "rows": r}

    size = rows // chunks
    drift_in = [
        pltpu.make_async_copy(
            drift_far.at[pl.ds(g * size, size)], drift.at[pl.ds(g * size, size)], dr_s.at[g]
        )
        for g in range(chunks)
    ]
    control_in = [
        pltpu.make_async_copy(control_far.at[j], control.at[j], co_s.at[j]) for j in range(nu)
    ]
    for copy in drift_in + control_in:
        copy.start()
    barrier = pltpu.get_barrier_semaphore()
    for d in peers:
        pl.semaphore_signal(barrier, inc=1, device_id=row_peer(d), device_id_type=MESH)
        pl.semaphore_signal(barrier, inc=1, device_id=line_peer(d), device_id_type=MESH)
    group_count = lax.axis_size("tm")
    side = {"tm": tm ^ 1, "rows": r}
    after = {"tm": lax.rem(tm + 1, group_count), "rows": r}
    ahead = {"tm": lax.rem(tm + group_count - 1, group_count), "rows": r}
    for device in (side, after, ahead):
        pl.semaphore_signal(barrier, inc=1, device_id=device, device_id_type=MESH)

    zs[0][pl.ds(r * rows, rows)] = start[...]
    eye = lax.broadcasted_iota(jnp.int32, (scen, scen), 0) == lax.broadcasted_iota(
        jnp.int32, (scen, scen), 1
    )
    lane = lax.broadcasted_iota(jnp.int32, (scen, width), 1)
    for k in range(steps):
        mixed = jnp.zeros((scen, width), F32)
        for j in range(nu):
            line = jnp.broadcast_to(ctl[k, j : j + 1, :], (scen, scen))
            column = jnp.sum(jnp.where(eye, line, 0.0), axis=1, keepdims=True)
            full = jnp.broadcast_to(column, (scen, width))
            wts[k, j] = full
            mixed = jnp.where(lane // span == j, full, mixed)
        wsend[k] = mixed
    pl.semaphore_wait(barrier, 9)
    pending = []

    def send(src, dst, s, t, to, keep=True):
        copy = pltpu.make_async_remote_copy(
            src_ref=src, dst_ref=dst, send_sem=s, recv_sem=t, device_id=to, device_id_type=MESH
        )
        copy.start()
        if keep:
            pending.append(copy)
        return copy

    def panel(k, row):
        return zs[k].at[pl.ds(row * rows, rows)]

    def far(k, e, row):
        return zfar.at[k, e - 1, pl.ds(row * rows, rows)]

    def gather_whole(k, d):
        return pltpu.make_async_remote_copy(
            src_ref=panel(k, r), dst_ref=panel(k, r), send_sem=ag_s.at[k, d - 1],
            recv_sem=ag_r.at[k, d - 1], device_id=row_peer(d), device_id_type=MESH,
        )

    def gather_part(k, g, d):
        part = zs[k].at[pl.ds(r * rows + g * size, size)]
        over = d == 2
        return pltpu.make_async_remote_copy(
            src_ref=part, dst_ref=part, send_sem=ay_s.at[k, g] if over else ag_s.at[k, d - 1],
            recv_sem=ay_r.at[k, g] if over else ag_r.at[k, d - 1], device_id=row_peer(d),
            device_id_type=MESH,
        )

    def gather_on(k, g):
        part = zs[k].at[pl.ds((r ^ 2) * rows + g * size, size)]
        return pltpu.make_async_remote_copy(
            src_ref=part, dst_ref=part, send_sem=af_s.at[k, g], recv_sem=ag_r.at[k, 2],
            device_id=row_peer(1), device_id_type=MESH,
        )

    inner = jnp.logical_or(q == 1, q == 2)

    def far_copy(k, e, row, s, t, to):
        there = far(k, e, row)
        return pltpu.make_async_remote_copy(
            src_ref=there, dst_ref=there, send_sem=s, recv_sem=t, device_id=to,
            device_id_type=MESH,
        )

    def line_copy(k, e):
        return pltpu.make_async_remote_copy(
            src_ref=panel(k, r), dst_ref=far(k, e, r), send_sem=zl_s.at[k, e - 1],
            recv_sem=zl_r.at[k, e - 1], device_id=line_peer(e), device_id_type=MESH,
        )

    def line_on(k):
        return pltpu.make_async_remote_copy(
            src_ref=far(k, 2, r), dst_ref=far(k, 3, r), send_sem=zq_s.at[k],
            recv_sem=zl_r.at[k, 2], device_id=line_peer(1), device_id_type=MESH,
        )

    def over_y(k, e):
        return far_copy(k, e, r, zy_s.at[k, e - 1], zy_r.at[k, e - 1], row_peer(2))

    def over_core(k, e, h):
        return far_copy(k, e, r ^ (2 * h), zc_s.at[k, e - 1, h], zc_r.at[k, e - 1, h], row_peer(1))

    def mu_copy(k, e):
        return pltpu.make_async_remote_copy(
            src_ref=muall.at[k, 0], dst_ref=muall.at[k, e], send_sem=mu_s.at[k, e - 1],
            recv_sem=mu_r.at[k, e - 1], device_id=line_peer(e), device_id_type=MESH,
        )

    def mu_part(g, e):
        part = pl.ds(g * size, size)
        return pltpu.make_async_remote_copy(
            src_ref=muall.at[0, 0, part], dst_ref=muall.at[0, e, part],
            send_sem=m0_s.at[g, e - 1], recv_sem=m0_r.at[g, e - 1], device_id=line_peer(e),
            device_id_type=MESH,
        )

    def mu_on(k):
        return pltpu.make_async_remote_copy(
            src_ref=muall.at[k, 2], dst_ref=muall.at[k, 3], send_sem=mq_s.at[k],
            recv_sem=mu_r.at[k, 2], device_id=line_peer(1), device_id_type=MESH,
        )

    def arrived(k, e):
        line_copy(k, e).wait_recv()
        over_core(k, e, 0).start()
        over_y(k, e).start()

    def crossed(k, e):
        over_y(k, e).wait_recv()
        over_core(k, e, 1).start()

    def move_states(t):
        if t < steps:
            line_copy(t, 2).start()
            pl.when(inner)(line_copy(t, 3).start)
            line_copy(t, 1).start()
        for k in range(steps):
            if t == k + 3:
                for e in (2, 1):
                    arrived(k, e)
                pl.when(inner)(line_on(k).start)
            if t == k + 4:
                arrived(k, 3)
                for e in (1, 2):
                    crossed(k, e)
            if t == k + 5:
                crossed(k, 3)

    for g in range(chunks):
        gather_part(0, g, 2).start()
    gather_whole(0, 1).start()
    gather_whole(0, 3).start()
    from_next = send(start, nxt, nb_s.at[0], nb_r.at[0], ahead)
    controls_in = [
        send(wsend, wfar.at[e - 1], wx_s.at[e - 1], wx_r.at[e - 1], line_peer(e)) for e in peers
    ]

    owner = jnp.concatenate(
        [dvec[m : m + 1, :] for m in range(slots)] + [cvec[j : j + 1, :] for j in range(nu)], 1
    )
    hits[...] = jnp.where(
        lax.broadcasted_iota(jnp.int32, (blocks, count), 0) == owner, 1.0, 0.0
    ).astype(BF16)
    prow = lax.broadcasted_iota(jnp.int32, (2 * width, width), 0)
    pcol = lax.broadcasted_iota(jnp.int32, (2 * width, width), 1)
    from_drift = lax.rem(prow + x * half, width)
    from_control = span * q + lax.rem(lax.rem(prow, span) + x * (span // 2), span)
    pick[...] = jnp.where(
        pcol == jnp.where(prow < width, from_drift, from_control), 1.0, 0.0
    ).astype(BF16)

    def turn_drift(i, carry):
        for m in range(slots):
            turned[i, pl.ds(m * width, width), :] = drift[i, m].T
        return carry

    for g in range(chunks):
        drift_in[g].wait()
        lax.fori_loop(g * size, (g + 1) * size, turn_drift, 0, unroll=4)
    for j in range(nu):
        control_in[j].wait()

        def turn_control(i, carry):
            turned[i, pl.ds((slots + j) * width, width), :] = control[j, i].T
            return carry

        lax.fori_loop(0, rows, turn_control, 0, unroll=8)

    for k in range(steps):
        for g in range(chunks):
            if k == 0 or g + 1 == chunks:
                gather_part(k, g, 2).wait_recv()
        gather_whole(k, 1).wait_recv()
        gather_whole(k, 3).wait_recv()
        move_states(k)

        def forward(i, carry):
            left = [zs[k][dcol[m, i]] for m in range(slots)]
            for j in range(nu):
                left.append((wts[k, j] * zs[k][ccol[j, i]].astype(F32)).astype(BF16))
            moved = jnp.dot(
                jnp.concatenate(left, 1), turned[i], preferred_element_type=F32
            ).astype(BF16)
            if k + 1 < steps:
                zs[k + 1][r * rows + i] = moved
            else:
                last[i] = moved
            return carry

        for g in range(chunks):
            lax.fori_loop(g * size, (g + 1) * size, forward, 0, unroll=True)
            if k + 1 < steps:
                for d in (2, 1) if g + 1 < chunks else (2, 3, 1):
                    gather_part(k + 1, g, d).start()
        if k + 1 < steps:
            for g in range(chunks - 1):
                gather_part(k + 1, g, 2).wait_recv()
                gather_on(k + 1, g).start()
    from_prev = send(last, before, nb_s.at[1], nb_r.at[1], after)
    from_next.wait_recv()
    ends = last[...].astype(F32)
    factor = jnp.where(tm < group_count - 1, defect_weight, 0.0)
    lam[...] = ends - tgt[steps - 1].astype(F32) - factor * (nxt[...].astype(F32) - ends)
    igt[...] = jnp.zeros((scen, width), F32)
    for k in reversed(range(steps)):
        muall[k, 0] = lam[...].astype(BF16)
        if k + 1 < steps:
            mu_copy(k + 1, 2).wait_recv()
            pl.when(inner)(mu_on(k + 1).start)
        if k > 0:
            pl.when(inner)(mu_copy(k, 3).start)
            mu_copy(k, 2).start()
            mu_copy(k, 1).start()
        else:
            for g in range(chunks):
                for e in (3, 2, 1):
                    mu_part(g, e).start()

        def backward(i, carry):
            right = [drift[i, m] for m in range(slots)] + [control[j, i] for j in range(nu)]
            back = jnp.dot(
                muall[k, 0, i], jnp.concatenate(right, 1), preferred_element_type=F32
            )
            for m in range(slots):
                terms[pl.ds(m * rows + i, scen, stride=count), :] = back[
                    :, m * width : (m + 1) * width
                ]
            sums = []
            for j in range(nu):
                at = (slots + j) * width
                term = back[:, at : at + width]
                sums.append(carry[j] + term * zs[k][ccol[j, i]].astype(F32))
                terms[pl.ds((slots + j) * rows + i, scen, stride=count), :] = wts[k, j] * term
            return tuple(sums)

        zero = jnp.zeros((scen, width), F32)
        sums = lax.fori_loop(0, rows, backward, (zero,) * nu, unroll=16)
        for s in range(scen):
            spread[pl.ds(s, blocks, stride=scen), :] = jnp.dot(
                hits[...], terms[pl.ds(s * count, count), :].astype(BF16),
                preferred_element_type=F32,
            )

        def share(row):
            at = pl.multiple_of(row * (rows * scen), rows * scen)
            return spread[pl.ds(at, rows * scen), :].reshape(rows, scen, width)

        arriving = []
        for d in (2, 3, 1):
            outbox[k, d - 1] = share(r ^ d).astype(BF16)
            arriving.append(
                send(outbox.at[k, d - 1], inbox.at[k, d - 1], rs_s.at[k, d - 1], rs_r.at[k, d - 1], row_peer(d))
            )
        for j in range(nu):
            column = jnp.sum(sums[j], axis=1, keepdims=True)
            igt[...] = jnp.where(lane == k * nu + j, column, igt[...])
        move_states(2 * steps - 1 - k)
        if k == 0:
            partial_in = [
                send(igt, igin.at[d - 1], ig_s.at[d - 1], ig_r.at[d - 1], row_peer(d))
                for d in peers
            ]
        if k == 0:
            break
        for copy in arriving:
            copy.wait_recv()
        total = share(r)
        for d in peers:
            total += inbox[k, d - 1].astype(F32)
        lam[...] = total + (zs[k][pl.ds(r * rows, rows)].astype(F32) - tgt[k - 1].astype(F32))
    for k in range(steps):
        for e in peers:
            if e != 2 and k > 0:
                mu_copy(k, e).wait_recv()
            for h in range(2):
                over_core(k, e, h).wait_recv()
    for copy in controls_in:
        copy.wait_recv()
    scale = (scen * steps * group_count) ** (-0.5)
    depth = steps * pairs * scen
    wide = []
    for k in range(steps):
        for e in range(pairs):
            wide.append(wsend[k] if e == 0 else wfar[e - 1, k])
    wall[...] = jnp.concatenate(wide, 0).T

    def picked(c):
        parts = []
        for k in range(steps):
            parts.append(zs[k][c])
            for e in range(pairs - 1):
                parts.append(zfar[k, e, c])
        return jnp.concatenate(parts, 0)

    def sums_of(i, carry):
        mu = jnp.concatenate([muall[k, e, i] for k in range(steps) for e in range(pairs)], 0)
        chosen = lax.dot_general(pick[...], mu, NT, preferred_element_type=F32)
        plain = chosen[:width].astype(BF16)
        weighted = (chosen[width:] * wall[...]).astype(BF16)
        block = jnp.dot(plain, picked(dcol[q, i]), preferred_element_type=F32) * scale
        own_d[i] = block[:half]
        xd_out[i] = block[half:].astype(BF16)
        for j in range(nu):
            block = (
                jnp.dot(
                    weighted[j * span : (j + 1) * span], picked(ccol[j, i]),
                    preferred_element_type=F32,
                )
                * scale
            )
            own_c[j, i] = block[: span // 2]
            xc_out[i, j] = block[span // 2 :].astype(BF16)
        return carry

    crossing = []
    per = rows // xd_s.shape[0]
    for g in range(xd_s.shape[0]):
        if g * per % size == 0:
            for e in peers:
                mu_part(g * per // size, e).wait_recv()
        lax.fori_loop(g * per, (g + 1) * per, sums_of, 0, unroll=True)
        part = pl.ds(g * per, per)
        crossing.append(
            (
                send(xd_out.at[part], xd_in.at[part], xd_s.at[g], xd_r.at[g], side),
                send(xc_out.at[part], xc_in.at[part], xc_s.at[g], xc_r.at[g], side),
            )
        )
    for copy in arriving:
        copy.wait_recv()
    total = share(r)
    for d in peers:
        total += inbox[0, d - 1].astype(F32)
    from_prev.wait_recv()
    back = jnp.where(tm > 0, defect_weight, 0.0)
    gshoot[...] = total + back * (start[...].astype(F32) - before[...].astype(F32))
    for copy in partial_in:
        copy.wait_recv()
    grads = igt[...] + igin[0] + igin[1] + igin[2]
    grads = jnp.concatenate([grads, jnp.zeros((width - scen, width), F32)], 0).T
    grads = grads * (blocks * width) ** (-0.5)
    for k in range(steps):
        gctl[k] = grads[k * nu : (k + 1) * nu, :scen]
    for one, two in crossing:
        one.wait_recv()
        two.wait_recv()
    for copy in pending:
        copy.wait_send()
    for k in range(steps):
        gather_whole(k, 1).wait_send()
        for g in range(chunks):
            gather_part(k, g, 2).wait_send()
            if k > 0 and g + 1 < chunks:
                gather_on(k, g).wait_send()
        if k > 0:
            gather_part(k, chunks - 1, 3).wait_send()
        else:
            gather_whole(k, 3).wait_send()
        for e in (1, 2):
            if k > 0:
                mu_copy(k, e).wait_send()
            line_copy(k, e).wait_send()
        pl.when(inner)(line_copy(k, 3).wait_send)
        pl.when(inner)(line_on(k).wait_send)
        for e in peers:
            over_y(k, e).wait_send()
            for h in range(2):
                over_core(k, e, h).wait_send()
        if k > 0:
            pl.when(inner)(mu_copy(k, 3).wait_send)
            pl.when(inner)(mu_on(k).wait_send)
    for g in range(chunks):
        for e in peers:
            mu_part(g, e).wait_send()


def finish_kernel(own_d, xd_in, own_c, xc_in, shoot_in, ctl_in, gdrift, gcontrol, gshoot, gctl):
    tile, half, _ = own_d.shape
    nu, deep = xc_in.shape[1], xc_in.shape[2]
    for i in range(tile):
        gdrift[pl.ds(i, half, stride=tile), :] = own_d[i] + xd_in[i].astype(F32)
        for j in range(nu):
            gcontrol[j, 0, pl.ds(i, deep, stride=tile), :] = own_c[j, i] + xc_in[i, j].astype(F32)
    gshoot[...] = shoot_in[...]
    gctl[...] = ctl_in[...]


def shards(
    drift_blocks, drift_cols, control_blocks, control_cols, controls, shooting_states, targets
):
    group_count, row_count = lax.axis_size("tm"), lax.axis_size("rows")
    rows, slots, width, _ = drift_blocks.shape
    nu = control_blocks.shape[0]
    steps, scen, local = targets.shape
    if not (
        group_count == 2 * slots and slots == 4 and nu == 4 and row_count == 4 and steps == 5
        and scen == 8 and width == 128 and rows == 32
    ):
        return general(
            drift_blocks, drift_cols, control_blocks, control_cols, controls, shooting_states,
            targets,
        )
    blocks = rows * row_count
    pairs = group_count // 2
    first = jnp.swapaxes(shooting_states[0].reshape(scen, rows, width), 0, 1)
    tgt = jnp.swapaxes(targets.reshape(steps, scen, rows, width), 1, 2)
    ctl = jnp.swapaxes(controls, 0, 1)
    cols = jnp.swapaxes(drift_cols, 0, 1)
    span = width // slots
    count = rows * (slots + nu)
    vmem = pl.BlockSpec(memory_space=pltpu.VMEM)
    smem = pl.BlockSpec(memory_space=pltpu.SMEM)
    anywhere = pl.BlockSpec(memory_space=pl.ANY)
    dma = pltpu.SemaphoreType.DMA
    groups = 8
    panel = (rows, scen, width)
    gshoot, gctl, own_d, own_c, xd_in, xc_in = pl.pallas_call(
        sweep_kernel,
        out_shape=(
            jax.ShapeDtypeStruct(panel, F32),
            jax.ShapeDtypeStruct((steps, nu, scen), F32),
            jax.ShapeDtypeStruct((rows, width // 2, width), F32),
            jax.ShapeDtypeStruct((nu, rows, span // 2, width), F32),
            jax.ShapeDtypeStruct((rows, width // 2, width), BF16),
            jax.ShapeDtypeStruct((rows, nu, span // 2, width), BF16),
        ),
        in_specs=[smem, smem, vmem, vmem, anywhere, anywhere, vmem, vmem, vmem],
        out_specs=(vmem,) * 6,
        scratch_shapes=[
            *[pltpu.VMEM((blocks, scen, width), BF16) for _ in range(5)],
            pltpu.VMEM((steps, pairs - 1, blocks, scen, width), BF16),
            pltpu.VMEM((steps, pairs, rows, scen, width), BF16),
            pltpu.VMEM((scen * count, width), F32),
            pltpu.VMEM((blocks * scen, width), F32),
            pltpu.VMEM((steps, 3, rows, scen, width), BF16),
            pltpu.VMEM((steps, 3, rows, scen, width), BF16),
            pltpu.VMEM(panel, F32),
            pltpu.VMEM(panel, BF16),
            pltpu.VMEM(panel, BF16),
            pltpu.VMEM(panel, BF16),
            pltpu.VMEM((steps, nu, scen, width), F32),
            pltpu.VMEM((blocks, count), BF16),
            pltpu.VMEM((scen, width), F32),
            pltpu.VMEM((3, scen, width), F32),
            pltpu.VMEM((steps, scen, width), F32),
            pltpu.VMEM((3, steps, scen, width), F32),
            pltpu.VMEM((width, steps * pairs * scen), F32),
            pltpu.VMEM((2 * width, width), BF16),
            pltpu.VMEM((rows, width // 2, width), BF16),
            pltpu.VMEM((rows, nu, span // 2, width), BF16),
            pltpu.VMEM(drift_blocks.shape, BF16),
            pltpu.VMEM(control_blocks.shape, BF16),
            pltpu.VMEM((rows, (slots + nu) * width, width), BF16),
            dma((4,)), dma((nu,)),
            dma((steps, 3)), dma((steps, 3)),
            dma((steps, 4)), dma((steps, 4)), dma((steps, 4)),
            dma((steps, 3)), dma((steps, 3)), dma((steps,)),
            dma((steps, 3)), dma((steps, 3)),
            dma((steps, 3, 2)), dma((steps, 3, 2)),
            dma((steps, 3)), dma((steps, 3)), dma((steps,)), dma((4, 3)), dma((4, 3)),
            dma((steps, 3)), dma((steps, 3)),
            dma((3,)), dma((3,)),
            dma((3,)), dma((3,)),
            dma((2,)), dma((2,)),
            dma((groups,)), dma((groups,)),
            dma((groups,)), dma((groups,)),
        ],
        compiler_params=pltpu.CompilerParams(
            collective_id=0, has_side_effects=True, vmem_limit_bytes=60 * 2**20
        ),
        name="sweep",
    )(cols, control_cols, cols, control_cols, drift_blocks, control_blocks, ctl, first, tgt)

    tile, half, deep = 8, width // 2, span // 2
    gdrift, gcontrol, gshoot, gctl = pl.pallas_call(
        finish_kernel,
        grid=(rows // tile,),
        out_shape=(
            jax.ShapeDtypeStruct((rows * half, width), F32),
            jax.ShapeDtypeStruct((nu, rows // tile, deep * tile, width), F32),
            jax.ShapeDtypeStruct(panel, F32),
            jax.ShapeDtypeStruct((steps, nu, scen), F32),
        ),
        in_specs=[
            pl.BlockSpec((tile, half, width), lambda g: (g, 0, 0)),
            pl.BlockSpec((tile, half, width), lambda g: (g, 0, 0)),
            pl.BlockSpec((nu, tile, deep, width), lambda g: (0, g, 0, 0)),
            pl.BlockSpec((tile, nu, deep, width), lambda g: (g, 0, 0, 0)),
            pl.BlockSpec((tile, scen, width), lambda g: (g, 0, 0)),
            pl.BlockSpec((steps, nu, scen), lambda g: (0, 0, 0)),
        ],
        out_specs=(
            pl.BlockSpec((half * tile, width), lambda g: (g, 0)),
            pl.BlockSpec((nu, 1, deep * tile, width), lambda g: (0, g, 0, 0)),
            pl.BlockSpec((tile, scen, width), lambda g: (g, 0, 0)),
            pl.BlockSpec((steps, nu, scen), lambda g: (0, 0, 0)),
        ),
        name="finish",
    )(own_d, xd_in, own_c, xc_in, gshoot, gctl)

    grad_shooting = jnp.swapaxes(gshoot, 0, 1).reshape(1, scen, local)
    grad_drift = gdrift.reshape(rows // 8, width // 2, 8, width)
    grad_control = gcontrol.reshape(nu, rows // 8, span // 2, 8, width)
    return (
        grad_shooting,
        jnp.swapaxes(gctl, 0, 1),
        jnp.swapaxes(grad_drift, 1, 2).reshape(rows, -1),
        jnp.swapaxes(grad_control, 2, 3).reshape(nu, rows, -1),
    )


def solution(mesh):
    return jax.shard_map(
        shards,
        mesh=mesh,
        in_specs=(
            P("rows", None, None, None),
            P("rows", None),
            P(None, "rows", None, None),
            P(None, "rows"),
            P(None, "tm", None),
            P("tm", None, "rows"),
            P("tm", None, "rows"),
        ),
        out_specs=(
            P("tm", None, "rows"),
            P(None, "tm", None),
            P("rows", "tm"),
            P(None, "rows", "tm"),
        ),
        check_vma=False,
    )
```

```python
import jax
import jax.numpy as jnp
from jax import lax
from jax.experimental import pallas as pl
from jax.experimental.pallas import tpu as pltpu
from jax.sharding import PartitionSpec as P

defect_weight = 2.0


def passed_along(value, axis, by):
    count = lax.axis_size(axis)
    pairs = [(i, i + by) for i in range(count) if 0 <= i + by < count]
    return lax.ppermute(value, axis, pairs)


def step_terms(gathered, block_width, drift_blocks, drift_cols, control_blocks, control_cols):
    blocks = gathered.reshape(gathered.shape[0], -1, block_width)
    total = jnp.arange(blocks.shape[1])
    drift_hits = (drift_cols[..., None] == total).astype(jnp.bfloat16)
    control_hits = (control_cols[..., None] == total).astype(jnp.bfloat16)
    picked = jnp.einsum(
        "nkb,sbi->snki", drift_hits, blocks, preferred_element_type=jnp.float32
    ).astype(jnp.bfloat16)
    drift_out = jnp.einsum(
        "snki,nkoi->sno", picked, drift_blocks, preferred_element_type=jnp.float32
    )
    control_picked = jnp.einsum(
        "jnb,sbi->sjni", control_hits, blocks, preferred_element_type=jnp.float32
    ).astype(jnp.bfloat16)
    control_out = jnp.einsum(
        "sjni,jnoi->sjno", control_picked, control_blocks, preferred_element_type=jnp.float32
    )
    return (picked, drift_out, control_picked, control_out)


def general(
    drift_blocks, drift_cols, control_blocks, control_cols, controls, shooting_states, targets
):
    block_width = drift_blocks.shape[-1]
    scenarios = shooting_states.shape[1]
    local_rows = shooting_states.shape[2]
    horizon_steps = targets.shape[0]
    group_count = lax.axis_size("tm")
    group_index = lax.axis_index("tm")
    total_blocks = drift_blocks.shape[0] * lax.axis_size("rows")
    lifted_total = local_rows * lax.axis_size("rows")
    operators = (drift_blocks, drift_cols, control_blocks, control_cols)
    row_count = lax.axis_size("rows")
    targets_of = jnp.concatenate([drift_cols.reshape(-1), control_cols.reshape(-1)])
    hits = (targets_of[:, None] == jnp.arange(total_blocks)[None]).astype(jnp.bfloat16)
    first_panel = shooting_states[0]
    panels = [first_panel]
    stored = []
    state_panel = first_panel
    for position in range(horizon_steps):
        gathered = lax.all_gather(state_panel, "rows", axis=1, tiled=True)
        step_parts = step_terms(gathered, block_width, *operators)
        stored.append(step_parts)
        weights = controls[:, position].T[:, :, None, None]
        mixed = step_parts[1] + jnp.sum(weights * step_parts[3], axis=1)
        state_panel = mixed.reshape(scenarios, local_rows).astype(jnp.bfloat16)
        panels.append(state_panel)
    group_end = panels[-1]
    next_start = passed_along(first_panel, "tm", -1)
    prev_end = passed_along(group_end, "tm", 1)
    end_wide = group_end.astype(jnp.float32)
    defect = jnp.where(
        group_index < group_count - 1, next_start.astype(jnp.float32) - end_wide, 0.0
    )
    prev_defect = jnp.where(
        group_index > 0, first_panel.astype(jnp.float32) - prev_end.astype(jnp.float32), 0.0
    )
    adjoint = end_wide - targets[horizon_steps - 1].astype(jnp.float32) - defect_weight * defect
    input_grads = [None] * horizon_steps
    mu_list = []
    picked_list = []
    weighted_list = []
    control_picked_list = []
    for position in reversed(range(horizon_steps)):
        adjoint_half = adjoint.astype(jnp.bfloat16)
        picked, drift_out, control_picked, control_out = stored[position]
        mu_blocks = adjoint_half.reshape(scenarios, -1, block_width)
        mu_wide = mu_blocks.astype(jnp.float32)
        weights = controls[:, position].T[:, :, None, None]
        input_grads[position] = jnp.sum(mu_wide[:, None] * control_out, axis=(2, 3)).T
        weighted = (mu_wide[:, None] * weights).astype(jnp.bfloat16)
        mu_list.append(mu_blocks)
        picked_list.append(picked)
        weighted_list.append(weighted)
        control_picked_list.append(control_picked)
        drift_back = jnp.einsum(
            "sno,nkoi->snki", mu_blocks, drift_blocks, preferred_element_type=jnp.float32
        )
        control_back = (
            jnp.einsum(
                "sno,jnoi->sjni", mu_blocks, control_blocks, preferred_element_type=jnp.float32
            )
            * weights
        )
        terms = jnp.concatenate(
            [
                drift_back.reshape(scenarios, -1, block_width),
                control_back.reshape(scenarios, -1, block_width),
            ],
            1,
        ).astype(jnp.bfloat16)
        spread = jnp.einsum("gc,sgi->csi", hits, terms, preferred_element_type=jnp.float32)
        spread = spread.astype(jnp.bfloat16).reshape(row_count, -1, scenarios, block_width)
        shares = lax.all_to_all(spread, "rows", 0, 0)
        total = jnp.sum(shares.astype(jnp.float32), 0)
        adjoint = jnp.swapaxes(total, 0, 1).reshape(scenarios, local_rows)
        if position > 0:
            adjoint = (
                adjoint
                + panels[position].astype(jnp.float32)
                - targets[position - 1].astype(jnp.float32)
            )
    grad_shooting = (adjoint + defect_weight * prev_defect)[None]
    grad_controls = lax.psum(jnp.stack(input_grads, 1), "rows") * lifted_total ** (-0.5)
    grad_scale = (scenarios * horizon_steps * group_count) ** (-0.5)
    all_mu = jnp.concatenate(mu_list, 0)
    all_picked = jnp.concatenate(picked_list, 0)
    drift_sum = jnp.einsum("sno,snki->nkoi", all_mu, all_picked, preferred_element_type=jnp.float32)
    all_weighted = jnp.concatenate(weighted_list, 0)
    all_control_picked = jnp.concatenate(control_picked_list, 0)
    control_sum = jnp.einsum(
        "sjno,sjni->jnoi", all_weighted, all_control_picked, preferred_element_type=jnp.float32
    )
    drift_flat = drift_sum.reshape(drift_sum.shape[0], -1)
    grad_drift = lax.psum_scatter(drift_flat, "tm", scatter_dimension=1, tiled=True) * grad_scale
    control_flat = control_sum.reshape(control_sum.shape[0], control_sum.shape[1], -1)
    grad_control_ops = (
        lax.psum_scatter(control_flat, "tm", scatter_dimension=2, tiled=True) * grad_scale
    )
    return (grad_shooting, grad_controls, grad_drift, grad_control_ops)


MESH = pl.DeviceIdType.MESH
F32, BF16 = jnp.float32, jnp.bfloat16


NT = (((1,), (1,)), ((), ()))


def sweep_kernel(
    dcol, ccol, dvec, cvec, drift_far, control_far, ctl, start, tgt,
    gshoot, gctl, own_d, own_c, xd_in, xc_in,
    z0, z1, z2, z3, z4, zfar, muall, terms, spread, outbox, inbox,
    lam, last, nxt, before, wts, hits, igt, igin, wsend, wfar, wall, pick,
    xd_out, xc_out, drift, control, turned,
    dr_s, co_s, ag_s, ag_r, ay_s, ay_r, af_s, zl_s, zl_r, zq_s, zy_s, zy_r, zc_s, zc_r, mu_s, mu_r, mq_s, m0_s, m0_r, rs_s, rs_r,
    ig_s, ig_r, wx_s, wx_r, nb_s, nb_r, xd_s, xd_r, xc_s, xc_r,
):
    zs = (z0, z1, z2, z3, z4)
    steps, blocks, scen, width = muall.shape[0], *zfar.shape[2:]
    pairs = muall.shape[1]
    rows = start.shape[0]
    slots, nu = drift.shape[1], control.shape[0]
    count = rows * (slots + nu)
    tm, r = lax.axis_index("tm"), lax.axis_index("rows")
    q, x = tm // 2, tm % 2
    peers = range(1, 4)
    chunks = 4
    span = width // slots
    half = width // 2

    def row_peer(d):
        return {"tm": tm, "rows": r ^ d}

    def line_peer(e):
        return {"tm": 2 * (q ^ e) + x, "rows": r}

    size = rows // chunks
    drift_in = [
        pltpu.make_async_copy(
            drift_far.at[pl.ds(g * size, size)], drift.at[pl.ds(g * size, size)], dr_s.at[g]
        )
        for g in range(chunks)
    ]
    control_in = [
        pltpu.make_async_copy(control_far.at[j], control.at[j], co_s.at[j]) for j in range(nu)
    ]
    for copy in drift_in + control_in:
        copy.start()
    barrier = pltpu.get_barrier_semaphore()
    for d in peers:
        pl.semaphore_signal(barrier, inc=1, device_id=row_peer(d), device_id_type=MESH)
        pl.semaphore_signal(barrier, inc=1, device_id=line_peer(d), device_id_type=MESH)
    group_count = lax.axis_size("tm")
    side = {"tm": tm ^ 1, "rows": r}
    after = {"tm": lax.rem(tm + 1, group_count), "rows": r}
    ahead = {"tm": lax.rem(tm + group_count - 1, group_count), "rows": r}
    for device in (side, after, ahead):
        pl.semaphore_signal(barrier, inc=1, device_id=device, device_id_type=MESH)

    zs[0][pl.ds(r * rows, rows)] = start[...]
    eye = lax.broadcasted_iota(jnp.int32, (scen, scen), 0) == lax.broadcasted_iota(
        jnp.int32, (scen, scen), 1
    )
    lane = lax.broadcasted_iota(jnp.int32, (scen, width), 1)
    for k in range(steps):
        mixed = jnp.zeros((scen, width), F32)
        for j in range(nu):
            line = jnp.broadcast_to(ctl[k, j : j + 1, :], (scen, scen))
            column = jnp.sum(jnp.where(eye, line, 0.0), axis=1, keepdims=True)
            full = jnp.broadcast_to(column, (scen, width))
            wts[k, j] = full
            mixed = jnp.where(lane // span == j, full, mixed)
        wsend[k] = mixed
    pl.semaphore_wait(barrier, 9)
    pending = []

    def send(src, dst, s, t, to, keep=True):
        copy = pltpu.make_async_remote_copy(
            src_ref=src, dst_ref=dst, send_sem=s, recv_sem=t, device_id=to, device_id_type=MESH
        )
        copy.start()
        if keep:
            pending.append(copy)
        return copy

    def panel(k, row):
        return zs[k].at[pl.ds(row * rows, rows)]

    def far(k, e, row):
        return zfar.at[k, e - 1, pl.ds(row * rows, rows)]

    def gather_whole(k, d):
        return pltpu.make_async_remote_copy(
            src_ref=panel(k, r), dst_ref=panel(k, r), send_sem=ag_s.at[k, d - 1],
            recv_sem=ag_r.at[k, d - 1], device_id=row_peer(d), device_id_type=MESH,
        )

    def gather_part(k, g, d):
        part = zs[k].at[pl.ds(r * rows + g * size, size)]
        over = d == 2
        return pltpu.make_async_remote_copy(
            src_ref=part, dst_ref=part, send_sem=ay_s.at[k, g] if over else ag_s.at[k, d - 1],
            recv_sem=ay_r.at[k, g] if over else ag_r.at[k, d - 1], device_id=row_peer(d),
            device_id_type=MESH,
        )

    def gather_on(k, g):
        part = zs[k].at[pl.ds((r ^ 2) * rows + g * size, size)]
        return pltpu.make_async_remote_copy(
            src_ref=part, dst_ref=part, send_sem=af_s.at[k, g], recv_sem=ag_r.at[k, 2],
            device_id=row_peer(1), device_id_type=MESH,
        )

    inner = jnp.logical_or(q == 1, q == 2)

    def far_copy(k, e, row, s, t, to):
        there = far(k, e, row)
        return pltpu.make_async_remote_copy(
            src_ref=there, dst_ref=there, send_sem=s, recv_sem=t, device_id=to,
            device_id_type=MESH,
        )

    def line_copy(k, e):
        return pltpu.make_async_remote_copy(
            src_ref=panel(k, r), dst_ref=far(k, e, r), send_sem=zl_s.at[k, e - 1],
            recv_sem=zl_r.at[k, e - 1], device_id=line_peer(e), device_id_type=MESH,
        )

    def line_on(k):
        return pltpu.make_async_remote_copy(
            src_ref=far(k, 2, r), dst_ref=far(k, 3, r), send_sem=zq_s.at[k],
            recv_sem=zl_r.at[k, 2], device_id=line_peer(1), device_id_type=MESH,
        )

    def over_y(k, e):
        return far_copy(k, e, r, zy_s.at[k, e - 1], zy_r.at[k, e - 1], row_peer(2))

    def over_core(k, e, h):
        return far_copy(k, e, r ^ (2 * h), zc_s.at[k, e - 1, h], zc_r.at[k, e - 1, h], row_peer(1))

    def mu_copy(k, e):
        return pltpu.make_async_remote_copy(
            src_ref=muall.at[k, 0], dst_ref=muall.at[k, e], send_sem=mu_s.at[k, e - 1],
            recv_sem=mu_r.at[k, e - 1], device_id=line_peer(e), device_id_type=MESH,
        )

    def mu_part(g, e):
        part = pl.ds(g * size, size)
        return pltpu.make_async_remote_copy(
            src_ref=muall.at[0, 0, part], dst_ref=muall.at[0, e, part],
            send_sem=m0_s.at[g, e - 1], recv_sem=m0_r.at[g, e - 1], device_id=line_peer(e),
            device_id_type=MESH,
        )

    def mu_on(k):
        return pltpu.make_async_remote_copy(
            src_ref=muall.at[k, 2], dst_ref=muall.at[k, 3], send_sem=mq_s.at[k],
            recv_sem=mu_r.at[k, 2], device_id=line_peer(1), device_id_type=MESH,
        )

    def arrived(k, e):
        line_copy(k, e).wait_recv()
        over_core(k, e, 0).start()
        over_y(k, e).start()

    def crossed(k, e):
        over_y(k, e).wait_recv()
        over_core(k, e, 1).start()

    def move_states(t):
        for k in range(steps):
            if t == k + 3:
                for e in (2, 1):
                    arrived(k, e)
                pl.when(inner)(line_on(k).start)
            if t == k + 4:
                arrived(k, 3)
                for e in (1, 2):
                    crossed(k, e)
            if t == k + 5:
                crossed(k, 3)

    for g in range(chunks):
        gather_part(0, g, 2).start()
    gather_whole(0, 1).start()
    gather_whole(0, 3).start()
    from_next = send(start, nxt, nb_s.at[0], nb_r.at[0], ahead)
    controls_in = [
        send(wsend, wfar.at[e - 1], wx_s.at[e - 1], wx_r.at[e - 1], line_peer(e)) for e in peers
    ]

    owner = jnp.concatenate(
        [dvec[m : m + 1, :] for m in range(slots)] + [cvec[j : j + 1, :] for j in range(nu)], 1
    )
    hits[...] = jnp.where(
        lax.broadcasted_iota(jnp.int32, (blocks, count), 0) == owner, 1.0, 0.0
    ).astype(BF16)
    prow = lax.broadcasted_iota(jnp.int32, (2 * width, width), 0)
    pcol = lax.broadcasted_iota(jnp.int32, (2 * width, width), 1)
    from_drift = lax.rem(prow + x * half, width)
    from_control = span * q + lax.rem(lax.rem(prow, span) + x * (span // 2), span)
    pick[...] = jnp.where(
        pcol == jnp.where(prow < width, from_drift, from_control), 1.0, 0.0
    ).astype(BF16)

    def turn_drift(i, carry):
        for m in range(slots):
            turned[i, pl.ds(m * width, width), :] = drift[i, m].T
        return carry

    for g in range(chunks):
        drift_in[g].wait()
        lax.fori_loop(g * size, (g + 1) * size, turn_drift, 0, unroll=4)
    for j in range(nu):
        control_in[j].wait()

        def turn_control(i, carry):
            turned[i, pl.ds((slots + j) * width, width), :] = control[j, i].T
            return carry

        lax.fori_loop(0, rows, turn_control, 0, unroll=8)

    for k in range(steps):
        for g in range(chunks):
            if k == 0 or g + 1 == chunks:
                gather_part(k, g, 2).wait_recv()
        gather_whole(k, 1).wait_recv()
        gather_whole(k, 3).wait_recv()
        line_copy(k, 2).start()
        pl.when(inner)(line_copy(k, 3).start)
        line_copy(k, 1).start()

        def forward(i, carry):
            left = [zs[k][dcol[m, i]] for m in range(slots)]
            for j in range(nu):
                left.append((wts[k, j] * zs[k][ccol[j, i]].astype(F32)).astype(BF16))
            moved = jnp.dot(
                jnp.concatenate(left, 1), turned[i], preferred_element_type=F32
            ).astype(BF16)
            if k + 1 < steps:
                zs[k + 1][r * rows + i] = moved
            else:
                last[i] = moved
            return carry

        for g in range(chunks):
            lax.fori_loop(g * size, (g + 1) * size, forward, 0, unroll=True)
            if k + 1 < steps:
                for d in (2, 1) if g + 1 < chunks else (2, 3, 1):
                    gather_part(k + 1, g, d).start()
        move_states(k)
        if k + 1 < steps:
            for g in range(chunks - 1):
                gather_part(k + 1, g, 2).wait_recv()
                gather_on(k + 1, g).start()
    from_prev = send(last, before, nb_s.at[1], nb_r.at[1], after)
    from_next.wait_recv()
    ends = last[...].astype(F32)
    factor = jnp.where(tm < group_count - 1, defect_weight, 0.0)
    lam[...] = ends - tgt[steps - 1].astype(F32) - factor * (nxt[...].astype(F32) - ends)
    igt[...] = jnp.zeros((scen, width), F32)
    for k in reversed(range(steps)):
        muall[k, 0] = lam[...].astype(BF16)
        if k + 1 < steps:
            mu_copy(k + 1, 2).wait_recv()
            pl.when(inner)(mu_on(k + 1).start)
        if k > 0:
            pl.when(inner)(mu_copy(k, 3).start)
            mu_copy(k, 2).start()
            mu_copy(k, 1).start()
        else:
            for g in range(chunks):
                for e in (3, 2, 1):
                    mu_part(g, e).start()

        def backward(i, carry):
            right = [drift[i, m] for m in range(slots)] + [control[j, i] for j in range(nu)]
            back = jnp.dot(
                muall[k, 0, i], jnp.concatenate(right, 1), preferred_element_type=F32
            )
            for m in range(slots):
                terms[pl.ds(m * rows + i, scen, stride=count), :] = back[
                    :, m * width : (m + 1) * width
                ]
            sums = []
            for j in range(nu):
                at = (slots + j) * width
                term = back[:, at : at + width]
                sums.append(carry[j] + term * zs[k][ccol[j, i]].astype(F32))
                terms[pl.ds((slots + j) * rows + i, scen, stride=count), :] = wts[k, j] * term
            return tuple(sums)

        zero = jnp.zeros((scen, width), F32)
        sums = lax.fori_loop(0, rows, backward, (zero,) * nu, unroll=16)
        for s in range(scen):
            spread[pl.ds(s, blocks, stride=scen), :] = jnp.dot(
                hits[...], terms[pl.ds(s * count, count), :].astype(BF16),
                preferred_element_type=F32,
            )

        def share(row):
            at = pl.multiple_of(row * (rows * scen), rows * scen)
            return spread[pl.ds(at, rows * scen), :].reshape(rows, scen, width)

        arriving = []
        for d in (2, 3, 1):
            outbox[k, d - 1] = share(r ^ d).astype(BF16)
            arriving.append(
                send(outbox.at[k, d - 1], inbox.at[k, d - 1], rs_s.at[k, d - 1], rs_r.at[k, d - 1], row_peer(d))
            )
        for j in range(nu):
            column = jnp.sum(sums[j], axis=1, keepdims=True)
            igt[...] = jnp.where(lane == k * nu + j, column, igt[...])
        move_states(2 * steps - 1 - k)
        if k == 0:
            partial_in = [
                send(igt, igin.at[d - 1], ig_s.at[d - 1], ig_r.at[d - 1], row_peer(d))
                for d in peers
            ]
        if k == 0:
            break
        for copy in arriving:
            copy.wait_recv()
        total = share(r)
        for d in peers:
            total += inbox[k, d - 1].astype(F32)
        lam[...] = total + (zs[k][pl.ds(r * rows, rows)].astype(F32) - tgt[k - 1].astype(F32))
    for k in range(steps):
        for e in peers:
            if e != 2 and k > 0:
                mu_copy(k, e).wait_recv()
            for h in range(2):
                over_core(k, e, h).wait_recv()
    for copy in controls_in:
        copy.wait_recv()
    scale = (scen * steps * group_count) ** (-0.5)
    depth = steps * pairs * scen
    wide = []
    for k in range(steps):
        for e in range(pairs):
            wide.append(wsend[k] if e == 0 else wfar[e - 1, k])
    wall[...] = jnp.concatenate(wide, 0).T

    def picked(c):
        parts = []
        for k in range(steps):
            parts.append(zs[k][c])
            for e in range(pairs - 1):
                parts.append(zfar[k, e, c])
        return jnp.concatenate(parts, 0)

    def sums_of(i, carry):
        mu = jnp.concatenate([muall[k, e, i] for k in range(steps) for e in range(pairs)], 0)
        chosen = lax.dot_general(pick[...], mu, NT, preferred_element_type=F32)
        plain = chosen[:width].astype(BF16)
        weighted = (chosen[width:] * wall[...]).astype(BF16)
        block = jnp.dot(plain, picked(dcol[q, i]), preferred_element_type=F32) * scale
        own_d[i] = block[:half]
        xd_out[i] = block[half:].astype(BF16)
        for j in range(nu):
            block = (
                jnp.dot(
                    weighted[j * span : (j + 1) * span], picked(ccol[j, i]),
                    preferred_element_type=F32,
                )
                * scale
            )
            own_c[j, i] = block[: span // 2]
            xc_out[i, j] = block[span // 2 :].astype(BF16)
        return carry

    crossing = []
    per = rows // xd_s.shape[0]
    for g in range(xd_s.shape[0]):
        if g * per % size == 0:
            for e in peers:
                mu_part(g * per // size, e).wait_recv()
        lax.fori_loop(g * per, (g + 1) * per, sums_of, 0, unroll=True)
        part = pl.ds(g * per, per)
        crossing.append(
            (
                send(xd_out.at[part], xd_in.at[part], xd_s.at[g], xd_r.at[g], side),
                send(xc_out.at[part], xc_in.at[part], xc_s.at[g], xc_r.at[g], side),
            )
        )
    for copy in arriving:
        copy.wait_recv()
    total = share(r)
    for d in peers:
        total += inbox[0, d - 1].astype(F32)
    from_prev.wait_recv()
    back = jnp.where(tm > 0, defect_weight, 0.0)
    gshoot[...] = total + back * (start[...].astype(F32) - before[...].astype(F32))
    for copy in partial_in:
        copy.wait_recv()
    grads = igt[...] + igin[0] + igin[1] + igin[2]
    grads = jnp.concatenate([grads, jnp.zeros((width - scen, width), F32)], 0).T
    grads = grads * (blocks * width) ** (-0.5)
    for k in range(steps):
        gctl[k] = grads[k * nu : (k + 1) * nu, :scen]
    for one, two in crossing:
        one.wait_recv()
        two.wait_recv()
    for copy in pending:
        copy.wait_send()
    for k in range(steps):
        gather_whole(k, 1).wait_send()
        for g in range(chunks):
            gather_part(k, g, 2).wait_send()
            if k > 0 and g + 1 < chunks:
                gather_on(k, g).wait_send()
        if k > 0:
            gather_part(k, chunks - 1, 3).wait_send()
        else:
            gather_whole(k, 3).wait_send()
        for e in (1, 2):
            if k > 0:
                mu_copy(k, e).wait_send()
            line_copy(k, e).wait_send()
        pl.when(inner)(line_copy(k, 3).wait_send)
        pl.when(inner)(line_on(k).wait_send)
        for e in peers:
            over_y(k, e).wait_send()
            for h in range(2):
                over_core(k, e, h).wait_send()
        if k > 0:
            pl.when(inner)(mu_copy(k, 3).wait_send)
            pl.when(inner)(mu_on(k).wait_send)
    for g in range(chunks):
        for e in peers:
            mu_part(g, e).wait_send()


def finish_kernel(own_d, xd_in, own_c, xc_in, shoot_in, ctl_in, gdrift, gcontrol, gshoot, gctl):
    rows, half, _ = own_d.shape
    nu, deep, tile = xc_in.shape[1], xc_in.shape[2], 8

    def whole(i, carry):
        group, within = i // tile, lax.rem(i, tile)
        gdrift[pl.ds(group * (half * tile) + within, half, stride=tile), :] = own_d[i] + xd_in[
            i
        ].astype(F32)
        for j in range(nu):
            at = (j * (rows // tile) + group) * (deep * tile) + within
            gcontrol[pl.ds(at, deep, stride=tile), :] = own_c[j, i] + xc_in[i, j].astype(F32)
        return carry

    lax.fori_loop(0, rows, whole, 0, unroll=8)
    gshoot[...] = shoot_in[...]
    gctl[...] = ctl_in[...]


def shards(
    drift_blocks, drift_cols, control_blocks, control_cols, controls, shooting_states, targets
):
    group_count, row_count = lax.axis_size("tm"), lax.axis_size("rows")
    rows, slots, width, _ = drift_blocks.shape
    nu = control_blocks.shape[0]
    steps, scen, local = targets.shape
    if not (
        group_count == 2 * slots and slots == 4 and nu == 4 and row_count == 4 and steps == 5
        and scen == 8 and width == 128 and rows == 32
    ):
        return general(
            drift_blocks, drift_cols, control_blocks, control_cols, controls, shooting_states,
            targets,
        )
    blocks = rows * row_count
    pairs = group_count // 2
    first = jnp.swapaxes(shooting_states[0].reshape(scen, rows, width), 0, 1)
    tgt = jnp.swapaxes(targets.reshape(steps, scen, rows, width), 1, 2)
    ctl = jnp.swapaxes(controls, 0, 1)
    cols = jnp.swapaxes(drift_cols, 0, 1)
    span = width // slots
    count = rows * (slots + nu)
    vmem = pl.BlockSpec(memory_space=pltpu.VMEM)
    smem = pl.BlockSpec(memory_space=pltpu.SMEM)
    anywhere = pl.BlockSpec(memory_space=pl.ANY)
    dma = pltpu.SemaphoreType.DMA
    groups = 8
    panel = (rows, scen, width)
    gshoot, gctl, own_d, own_c, xd_in, xc_in = pl.pallas_call(
        sweep_kernel,
        out_shape=(
            pltpu.VMEM(panel, F32),
            pltpu.VMEM((steps, nu, scen), F32),
            pltpu.VMEM((rows, width // 2, width), F32),
            pltpu.VMEM((nu, rows, span // 2, width), F32),
            pltpu.VMEM((rows, width // 2, width), BF16),
            pltpu.VMEM((rows, nu, span // 2, width), BF16),
        ),
        in_specs=[smem, smem, vmem, vmem, anywhere, anywhere, vmem, vmem, vmem],
        out_specs=(vmem,) * 6,
        scratch_shapes=[
            *[pltpu.VMEM((blocks, scen, width), BF16) for _ in range(5)],
            pltpu.VMEM((steps, pairs - 1, blocks, scen, width), BF16),
            pltpu.VMEM((steps, pairs, rows, scen, width), BF16),
            pltpu.VMEM((scen * count, width), F32),
            pltpu.VMEM((blocks * scen, width), F32),
            pltpu.VMEM((steps, 3, rows, scen, width), BF16),
            pltpu.VMEM((steps, 3, rows, scen, width), BF16),
            pltpu.VMEM(panel, F32),
            pltpu.VMEM(panel, BF16),
            pltpu.VMEM(panel, BF16),
            pltpu.VMEM(panel, BF16),
            pltpu.VMEM((steps, nu, scen, width), F32),
            pltpu.VMEM((blocks, count), BF16),
            pltpu.VMEM((scen, width), F32),
            pltpu.VMEM((3, scen, width), F32),
            pltpu.VMEM((steps, scen, width), F32),
            pltpu.VMEM((3, steps, scen, width), F32),
            pltpu.VMEM((width, steps * pairs * scen), F32),
            pltpu.VMEM((2 * width, width), BF16),
            pltpu.VMEM((rows, width // 2, width), BF16),
            pltpu.VMEM((rows, nu, span // 2, width), BF16),
            pltpu.VMEM(drift_blocks.shape, BF16),
            pltpu.VMEM(control_blocks.shape, BF16),
            pltpu.VMEM((rows, (slots + nu) * width, width), BF16),
            dma((4,)), dma((nu,)),
            dma((steps, 3)), dma((steps, 3)),
            dma((steps, 4)), dma((steps, 4)), dma((steps, 4)),
            dma((steps, 3)), dma((steps, 3)), dma((steps,)),
            dma((steps, 3)), dma((steps, 3)),
            dma((steps, 3, 2)), dma((steps, 3, 2)),
            dma((steps, 3)), dma((steps, 3)), dma((steps,)), dma((4, 3)), dma((4, 3)),
            dma((steps, 3)), dma((steps, 3)),
            dma((3,)), dma((3,)),
            dma((3,)), dma((3,)),
            dma((2,)), dma((2,)),
            dma((groups,)), dma((groups,)),
            dma((groups,)), dma((groups,)),
        ],
        compiler_params=pltpu.CompilerParams(
            collective_id=0, has_side_effects=True, vmem_limit_bytes=52 * 2**20
        ),
        name="sweep",
    )(cols, control_cols, cols, control_cols, drift_blocks, control_blocks, ctl, first, tgt)

    gdrift, gcontrol, gshoot, gctl = pl.pallas_call(
        finish_kernel,
        out_shape=(
            jax.ShapeDtypeStruct((rows * width // 2, width), F32),
            jax.ShapeDtypeStruct((nu * rows * span // 2, width), F32),
            jax.ShapeDtypeStruct(panel, F32),
            jax.ShapeDtypeStruct((steps, nu, scen), F32),
        ),
        in_specs=[vmem] * 6,
        out_specs=(vmem,) * 4,
        name="finish",
    )(*[pltpu.with_memory_space_constraint(v, pltpu.VMEM) for v in (own_d, xd_in, own_c, xc_in, gshoot, gctl)])

    grad_shooting = jnp.swapaxes(gshoot, 0, 1).reshape(1, scen, local)
    grad_drift = gdrift.reshape(rows // 8, width // 2, 8, width)
    grad_control = gcontrol.reshape(nu, rows // 8, span // 2, 8, width)
    return (
        grad_shooting,
        jnp.swapaxes(gctl, 0, 1),
        jnp.swapaxes(grad_drift, 1, 2).reshape(rows, -1),
        jnp.swapaxes(grad_control, 2, 3).reshape(nu, rows, -1),
    )


def solution(mesh):
    return jax.shard_map(
        shards,
        mesh=mesh,
        in_specs=(
            P("rows", None, None, None),
            P("rows", None),
            P(None, "rows", None, None),
            P(None, "rows"),
            P(None, "tm", None),
            P("tm", None, "rows"),
            P("tm", None, "rows"),
        ),
        out_specs=(
            P("tm", None, "rows"),
            P(None, "tm", None),
            P("rows", "tm"),
            P(None, "rows", "tm"),
        ),
        check_vma=False,
    )
```

```python
import jax
import jax.numpy as jnp
from jax import lax
from jax.experimental import pallas as pl
from jax.experimental.pallas import tpu as pltpu
from jax.sharding import PartitionSpec as P

defect_weight = 2.0


def passed_along(value, axis, by):
    count = lax.axis_size(axis)
    pairs = [(i, i + by) for i in range(count) if 0 <= i + by < count]
    return lax.ppermute(value, axis, pairs)


def step_terms(gathered, block_width, drift_blocks, drift_cols, control_blocks, control_cols):
    blocks = gathered.reshape(gathered.shape[0], -1, block_width)
    total = jnp.arange(blocks.shape[1])
    drift_hits = (drift_cols[..., None] == total).astype(jnp.bfloat16)
    control_hits = (control_cols[..., None] == total).astype(jnp.bfloat16)
    picked = jnp.einsum(
        "nkb,sbi->snki", drift_hits, blocks, preferred_element_type=jnp.float32
    ).astype(jnp.bfloat16)
    drift_out = jnp.einsum(
        "snki,nkoi->sno", picked, drift_blocks, preferred_element_type=jnp.float32
    )
    control_picked = jnp.einsum(
        "jnb,sbi->sjni", control_hits, blocks, preferred_element_type=jnp.float32
    ).astype(jnp.bfloat16)
    control_out = jnp.einsum(
        "sjni,jnoi->sjno", control_picked, control_blocks, preferred_element_type=jnp.float32
    )
    return (picked, drift_out, control_picked, control_out)


def general(
    drift_blocks, drift_cols, control_blocks, control_cols, controls, shooting_states, targets
):
    block_width = drift_blocks.shape[-1]
    scenarios = shooting_states.shape[1]
    local_rows = shooting_states.shape[2]
    horizon_steps = targets.shape[0]
    group_count = lax.axis_size("tm")
    group_index = lax.axis_index("tm")
    total_blocks = drift_blocks.shape[0] * lax.axis_size("rows")
    lifted_total = local_rows * lax.axis_size("rows")
    operators = (drift_blocks, drift_cols, control_blocks, control_cols)
    row_count = lax.axis_size("rows")
    targets_of = jnp.concatenate([drift_cols.reshape(-1), control_cols.reshape(-1)])
    hits = (targets_of[:, None] == jnp.arange(total_blocks)[None]).astype(jnp.bfloat16)
    first_panel = shooting_states[0]
    panels = [first_panel]
    stored = []
    state_panel = first_panel
    for position in range(horizon_steps):
        gathered = lax.all_gather(state_panel, "rows", axis=1, tiled=True)
        step_parts = step_terms(gathered, block_width, *operators)
        stored.append(step_parts)
        weights = controls[:, position].T[:, :, None, None]
        mixed = step_parts[1] + jnp.sum(weights * step_parts[3], axis=1)
        state_panel = mixed.reshape(scenarios, local_rows).astype(jnp.bfloat16)
        panels.append(state_panel)
    group_end = panels[-1]
    next_start = passed_along(first_panel, "tm", -1)
    prev_end = passed_along(group_end, "tm", 1)
    end_wide = group_end.astype(jnp.float32)
    defect = jnp.where(
        group_index < group_count - 1, next_start.astype(jnp.float32) - end_wide, 0.0
    )
    prev_defect = jnp.where(
        group_index > 0, first_panel.astype(jnp.float32) - prev_end.astype(jnp.float32), 0.0
    )
    adjoint = end_wide - targets[horizon_steps - 1].astype(jnp.float32) - defect_weight * defect
    input_grads = [None] * horizon_steps
    mu_list = []
    picked_list = []
    weighted_list = []
    control_picked_list = []
    for position in reversed(range(horizon_steps)):
        adjoint_half = adjoint.astype(jnp.bfloat16)
        picked, drift_out, control_picked, control_out = stored[position]
        mu_blocks = adjoint_half.reshape(scenarios, -1, block_width)
        mu_wide = mu_blocks.astype(jnp.float32)
        weights = controls[:, position].T[:, :, None, None]
        input_grads[position] = jnp.sum(mu_wide[:, None] * control_out, axis=(2, 3)).T
        weighted = (mu_wide[:, None] * weights).astype(jnp.bfloat16)
        mu_list.append(mu_blocks)
        picked_list.append(picked)
        weighted_list.append(weighted)
        control_picked_list.append(control_picked)
        drift_back = jnp.einsum(
            "sno,nkoi->snki", mu_blocks, drift_blocks, preferred_element_type=jnp.float32
        )
        control_back = (
            jnp.einsum(
                "sno,jnoi->sjni", mu_blocks, control_blocks, preferred_element_type=jnp.float32
            )
            * weights
        )
        terms = jnp.concatenate(
            [
                drift_back.reshape(scenarios, -1, block_width),
                control_back.reshape(scenarios, -1, block_width),
            ],
            1,
        ).astype(jnp.bfloat16)
        spread = jnp.einsum("gc,sgi->csi", hits, terms, preferred_element_type=jnp.float32)
        spread = spread.astype(jnp.bfloat16).reshape(row_count, -1, scenarios, block_width)
        shares = lax.all_to_all(spread, "rows", 0, 0)
        total = jnp.sum(shares.astype(jnp.float32), 0)
        adjoint = jnp.swapaxes(total, 0, 1).reshape(scenarios, local_rows)
        if position > 0:
            adjoint = (
                adjoint
                + panels[position].astype(jnp.float32)
                - targets[position - 1].astype(jnp.float32)
            )
    grad_shooting = (adjoint + defect_weight * prev_defect)[None]
    grad_controls = lax.psum(jnp.stack(input_grads, 1), "rows") * lifted_total ** (-0.5)
    grad_scale = (scenarios * horizon_steps * group_count) ** (-0.5)
    all_mu = jnp.concatenate(mu_list, 0)
    all_picked = jnp.concatenate(picked_list, 0)
    drift_sum = jnp.einsum("sno,snki->nkoi", all_mu, all_picked, preferred_element_type=jnp.float32)
    all_weighted = jnp.concatenate(weighted_list, 0)
    all_control_picked = jnp.concatenate(control_picked_list, 0)
    control_sum = jnp.einsum(
        "sjno,sjni->jnoi", all_weighted, all_control_picked, preferred_element_type=jnp.float32
    )
    drift_flat = drift_sum.reshape(drift_sum.shape[0], -1)
    grad_drift = lax.psum_scatter(drift_flat, "tm", scatter_dimension=1, tiled=True) * grad_scale
    control_flat = control_sum.reshape(control_sum.shape[0], control_sum.shape[1], -1)
    grad_control_ops = (
        lax.psum_scatter(control_flat, "tm", scatter_dimension=2, tiled=True) * grad_scale
    )
    return (grad_shooting, grad_controls, grad_drift, grad_control_ops)


MESH = pl.DeviceIdType.MESH
F32, BF16 = jnp.float32, jnp.bfloat16


NT = (((1,), (1,)), ((), ()))


def sweep_kernel(
    dcol, ccol, dvec, cvec, drift_far, control_far, ctl, start, tgt,
    gshoot, gctl, own_d, own_c, xd_in, xc_in,
    z0, z1, z2, z3, z4, zfar, muall, terms, spread, outbox, inbox,
    lam, last, nxt, before, wts, hits, igt, igin, wsend, wfar, wall, pick,
    xd_out, xc_out, drift, control, turned,
    dr_s, co_s, ag_s, ag_r, ay_s, ay_r, af_s, zl_s, zl_r, zq_s, zy_s, zy_r, zc_s, zc_r, mu_s, mu_r, mq_s, m0_s, m0_r, rs_s, rs_r,
    ig_s, ig_r, wx_s, wx_r, nb_s, nb_r, xd_s, xd_r, xc_s, xc_r,
):
    zs = (z0, z1, z2, z3, z4)
    steps, blocks, scen, width = muall.shape[0], *zfar.shape[2:]
    pairs = muall.shape[1]
    rows = start.shape[0]
    slots, nu = drift.shape[1], control.shape[0]
    count = rows * (slots + nu)
    tm, r = lax.axis_index("tm"), lax.axis_index("rows")
    q, x = tm // 2, tm % 2
    peers = range(1, 4)
    chunks = 4
    span = width // slots
    half = width // 2

    def row_peer(d):
        return {"tm": tm, "rows": r ^ d}

    def line_peer(e):
        return {"tm": 2 * (q ^ e) + x, "rows": r}

    size = rows // chunks
    drift_in = [
        pltpu.make_async_copy(
            drift_far.at[pl.ds(g * size, size)], drift.at[pl.ds(g * size, size)], dr_s.at[g]
        )
        for g in range(chunks)
    ]
    control_in = [
        pltpu.make_async_copy(control_far.at[j], control.at[j], co_s.at[j]) for j in range(nu)
    ]
    for copy in drift_in + control_in:
        copy.start()
    barrier = pltpu.get_barrier_semaphore()
    for d in peers:
        pl.semaphore_signal(barrier, inc=1, device_id=row_peer(d), device_id_type=MESH)
        pl.semaphore_signal(barrier, inc=1, device_id=line_peer(d), device_id_type=MESH)
    group_count = lax.axis_size("tm")
    side = {"tm": tm ^ 1, "rows": r}
    after = {"tm": lax.rem(tm + 1, group_count), "rows": r}
    ahead = {"tm": lax.rem(tm + group_count - 1, group_count), "rows": r}
    for device in (side, after, ahead):
        pl.semaphore_signal(barrier, inc=1, device_id=device, device_id_type=MESH)

    zs[0][pl.ds(r * rows, rows)] = start[...]
    eye = lax.broadcasted_iota(jnp.int32, (scen, scen), 0) == lax.broadcasted_iota(
        jnp.int32, (scen, scen), 1
    )
    lane = lax.broadcasted_iota(jnp.int32, (scen, width), 1)
    for k in range(steps):
        mixed = jnp.zeros((scen, width), F32)
        for j in range(nu):
            line = jnp.broadcast_to(ctl[k, j : j + 1, :], (scen, scen))
            column = jnp.sum(jnp.where(eye, line, 0.0), axis=1, keepdims=True)
            full = jnp.broadcast_to(column, (scen, width))
            wts[k, j] = full
            mixed = jnp.where(lane // span == j, full, mixed)
        wsend[k] = mixed
    pl.semaphore_wait(barrier, 9)
    pending = []

    def send(src, dst, s, t, to, keep=True):
        copy = pltpu.make_async_remote_copy(
            src_ref=src, dst_ref=dst, send_sem=s, recv_sem=t, device_id=to, device_id_type=MESH
        )
        copy.start()
        if keep:
            pending.append(copy)
        return copy

    def panel(k, row):
        return zs[k].at[pl.ds(row * rows, rows)]

    def far(k, e, row):
        return zfar.at[k, e - 1, pl.ds(row * rows, rows)]

    def gather_whole(k, d):
        return pltpu.make_async_remote_copy(
            src_ref=panel(k, r), dst_ref=panel(k, r), send_sem=ag_s.at[k, d - 1],
            recv_sem=ag_r.at[k, d - 1], device_id=row_peer(d), device_id_type=MESH,
        )

    def gather_part(k, g, d):
        part = zs[k].at[pl.ds(r * rows + g * size, size)]
        over = d == 2
        return pltpu.make_async_remote_copy(
            src_ref=part, dst_ref=part, send_sem=ay_s.at[k, g] if over else ag_s.at[k, d - 1],
            recv_sem=ay_r.at[k, g] if over else ag_r.at[k, d - 1], device_id=row_peer(d),
            device_id_type=MESH,
        )

    def gather_on(k, g):
        part = zs[k].at[pl.ds((r ^ 2) * rows + g * size, size)]
        return pltpu.make_async_remote_copy(
            src_ref=part, dst_ref=part, send_sem=af_s.at[k, g], recv_sem=ag_r.at[k, 2],
            device_id=row_peer(1), device_id_type=MESH,
        )

    inner = jnp.logical_or(q == 1, q == 2)

    def far_copy(k, e, row, s, t, to):
        there = far(k, e, row)
        return pltpu.make_async_remote_copy(
            src_ref=there, dst_ref=there, send_sem=s, recv_sem=t, device_id=to,
            device_id_type=MESH,
        )

    def line_copy(k, e):
        return pltpu.make_async_remote_copy(
            src_ref=panel(k, r), dst_ref=far(k, e, r), send_sem=zl_s.at[k, e - 1],
            recv_sem=zl_r.at[k, e - 1], device_id=line_peer(e), device_id_type=MESH,
        )

    def line_on(k):
        return pltpu.make_async_remote_copy(
            src_ref=far(k, 2, r), dst_ref=far(k, 3, r), send_sem=zq_s.at[k],
            recv_sem=zl_r.at[k, 2], device_id=line_peer(1), device_id_type=MESH,
        )

    def over_y(k, e):
        return far_copy(k, e, r, zy_s.at[k, e - 1], zy_r.at[k, e - 1], row_peer(2))

    def over_core(k, e, h):
        return far_copy(k, e, r ^ (2 * h), zc_s.at[k, e - 1, h], zc_r.at[k, e - 1, h], row_peer(1))

    def mu_copy(k, e):
        return pltpu.make_async_remote_copy(
            src_ref=muall.at[k, 0], dst_ref=muall.at[k, e], send_sem=mu_s.at[k, e - 1],
            recv_sem=mu_r.at[k, e - 1], device_id=line_peer(e), device_id_type=MESH,
        )

    def mu_part(g, e):
        part = pl.ds(g * size, size)
        return pltpu.make_async_remote_copy(
            src_ref=muall.at[0, 0, part], dst_ref=muall.at[0, e, part],
            send_sem=m0_s.at[g, e - 1], recv_sem=m0_r.at[g, e - 1], device_id=line_peer(e),
            device_id_type=MESH,
        )

    def mu_on(k):
        return pltpu.make_async_remote_copy(
            src_ref=muall.at[k, 2], dst_ref=muall.at[k, 3], send_sem=mq_s.at[k],
            recv_sem=mu_r.at[k, 2], device_id=line_peer(1), device_id_type=MESH,
        )

    def arrived(k, e):
        line_copy(k, e).wait_recv()
        over_core(k, e, 0).start()
        over_y(k, e).start()

    def crossed(k, e):
        over_y(k, e).wait_recv()
        over_core(k, e, 1).start()

    def move_states(t):
        for k in range(steps):
            if t == k + 3:
                for e in (2, 1):
                    arrived(k, e)
                pl.when(inner)(line_on(k).start)
            if t == k + 4:
                arrived(k, 3)
                for e in (1, 2):
                    crossed(k, e)
            if t == k + 5:
                crossed(k, 3)

    for g in range(chunks):
        gather_part(0, g, 2).start()
    gather_whole(0, 1).start()
    gather_whole(0, 3).start()
    from_next = send(start, nxt, nb_s.at[0], nb_r.at[0], ahead)
    controls_in = [
        send(wsend, wfar.at[e - 1], wx_s.at[e - 1], wx_r.at[e - 1], line_peer(e)) for e in peers
    ]

    owner = jnp.concatenate(
        [dvec[m : m + 1, :] for m in range(slots)] + [cvec[j : j + 1, :] for j in range(nu)], 1
    )
    hits[...] = jnp.where(
        lax.broadcasted_iota(jnp.int32, (blocks, count), 0) == owner, 1.0, 0.0
    ).astype(BF16)
    prow = lax.broadcasted_iota(jnp.int32, (2 * width, width), 0)
    pcol = lax.broadcasted_iota(jnp.int32, (2 * width, width), 1)
    from_drift = lax.rem(prow + x * half, width)
    from_control = span * q + lax.rem(lax.rem(prow, span) + x * (span // 2), span)
    pick[...] = jnp.where(
        pcol == jnp.where(prow < width, from_drift, from_control), 1.0, 0.0
    ).astype(BF16)

    def turn_drift(i, carry):
        for m in range(slots):
            turned[i, pl.ds(m * width, width), :] = drift[i, m].T
        return carry

    for g in range(chunks):
        drift_in[g].wait()
        lax.fori_loop(g * size, (g + 1) * size, turn_drift, 0, unroll=4)
    for j in range(nu):
        control_in[j].wait()

        def turn_control(i, carry):
            turned[i, pl.ds((slots + j) * width, width), :] = control[j, i].T
            return carry

        lax.fori_loop(0, rows, turn_control, 0, unroll=8)

    for k in range(steps):
        for g in range(chunks):
            if k == 0 or g + 1 == chunks:
                gather_part(k, g, 2).wait_recv()
        gather_whole(k, 1).wait_recv()
        gather_whole(k, 3).wait_recv()
        line_copy(k, 2).start()
        pl.when(inner)(line_copy(k, 3).start)
        line_copy(k, 1).start()

        def forward(i, carry):
            left = [zs[k][dcol[m, i]] for m in range(slots)]
            for j in range(nu):
                left.append((wts[k, j] * zs[k][ccol[j, i]].astype(F32)).astype(BF16))
            moved = jnp.dot(
                jnp.concatenate(left, 1), turned[i], preferred_element_type=F32
            ).astype(BF16)
            if k + 1 < steps:
                zs[k + 1][r * rows + i] = moved
            else:
                last[i] = moved
            return carry

        for g in range(chunks):
            lax.fori_loop(g * size, (g + 1) * size, forward, 0, unroll=True)
            if k + 1 < steps:
                for d in (2, 1) if g + 1 < chunks else (2, 3, 1):
                    gather_part(k + 1, g, d).start()
        move_states(k)
        if k + 1 < steps:
            for g in range(chunks - 1):
                gather_part(k + 1, g, 2).wait_recv()
                gather_on(k + 1, g).start()
    from_prev = send(last, before, nb_s.at[1], nb_r.at[1], after)
    from_next.wait_recv()
    ends = last[...].astype(F32)
    factor = jnp.where(tm < group_count - 1, defect_weight, 0.0)
    lam[...] = ends - tgt[steps - 1].astype(F32) - factor * (nxt[...].astype(F32) - ends)
    igt[...] = jnp.zeros((scen, width), F32)
    def share(row):
        at = pl.multiple_of(row * (rows * scen), rows * scen)
        return spread[pl.ds(at, rows * scen), :].reshape(rows, scen, width)

    def send_share(k, d):
        outbox[k, d - 1] = share(r ^ d).astype(BF16)
        arriving.append(
            send(
                outbox.at[k, d - 1], inbox.at[k, d - 1], rs_s.at[k, d - 1], rs_r.at[k, d - 1],
                row_peer(d),
            )
        )

    for k in reversed(range(steps)):
        arriving = []
        muall[k, 0] = lam[...].astype(BF16)
        if k + 1 < steps:
            mu_copy(k + 1, 2).wait_recv()
            pl.when(inner)(mu_on(k + 1).start)
        if k > 0:
            pl.when(inner)(mu_copy(k, 3).start)
            mu_copy(k, 2).start()
            mu_copy(k, 1).start()
        else:
            for g in range(chunks):
                for e in (3, 2, 1):
                    mu_part(g, e).start()

        def backward(i, carry):
            right = [drift[i, m] for m in range(slots)] + [control[j, i] for j in range(nu)]
            back = jnp.dot(
                muall[k, 0, i], jnp.concatenate(right, 1), preferred_element_type=F32
            )
            for m in range(slots):
                terms[pl.ds(m * rows + i, scen, stride=count), :] = back[
                    :, m * width : (m + 1) * width
                ]
            sums = []
            for j in range(nu):
                at = (slots + j) * width
                term = back[:, at : at + width]
                sums.append(carry[j] + term * zs[k][ccol[j, i]].astype(F32))
                terms[pl.ds((slots + j) * rows + i, scen, stride=count), :] = wts[k, j] * term
            return tuple(sums)

        zero = jnp.zeros((scen, width), F32)
        sums = lax.fori_loop(0, rows, backward, (zero,) * nu, unroll=True)
        halves = [
            terms[pl.ds(s * count, count), :].astype(BF16) for s in range(scen)
        ]
        for pair in (1, 0):
            at = pl.multiple_of(((r // 2) ^ pair) * (2 * rows), 2 * rows)
            for s in range(scen):
                spread[pl.ds(at * scen + s, 2 * rows, stride=scen), :] = jnp.dot(
                    hits[pl.ds(at, 2 * rows), :], halves[s], preferred_element_type=F32
                )
            if pair == 1:
                send_share(k, 2)
                send_share(k, 3)
        send_share(k, 1)

        for j in range(nu):
            column = jnp.sum(sums[j], axis=1, keepdims=True)
            igt[...] = jnp.where(lane == k * nu + j, column, igt[...])
        move_states(2 * steps - 1 - k)
        if k == 0:
            partial_in = [
                send(igt, igin.at[d - 1], ig_s.at[d - 1], ig_r.at[d - 1], row_peer(d))
                for d in peers
            ]
        if k == 0:
            break
        for copy in arriving:
            copy.wait_recv()
        total = share(r)
        for d in peers:
            total += inbox[k, d - 1].astype(F32)
        lam[...] = total + (zs[k][pl.ds(r * rows, rows)].astype(F32) - tgt[k - 1].astype(F32))
    for k in range(steps):
        for e in peers:
            if e != 2 and k > 0:
                mu_copy(k, e).wait_recv()
            for h in range(2):
                over_core(k, e, h).wait_recv()
    for copy in controls_in:
        copy.wait_recv()
    scale = (scen * steps * group_count) ** (-0.5)
    depth = steps * pairs * scen
    wide = []
    for k in range(steps):
        for e in range(pairs):
            wide.append(wsend[k] if e == 0 else wfar[e - 1, k])
    wall[...] = jnp.concatenate(wide, 0).T

    def picked(c):
        parts = []
        for k in range(steps):
            parts.append(zs[k][c])
            for e in range(pairs - 1):
                parts.append(zfar[k, e, c])
        return jnp.concatenate(parts, 0)

    def sums_of(i, carry):
        mu = jnp.concatenate([muall[k, e, i] for k in range(steps) for e in range(pairs)], 0)
        chosen = lax.dot_general(pick[...], mu, NT, preferred_element_type=F32)
        plain = chosen[:width].astype(BF16)
        weighted = (chosen[width:] * wall[...]).astype(BF16)
        block = jnp.dot(plain, picked(dcol[q, i]), preferred_element_type=F32) * scale
        own_d[i] = block[:half]
        xd_out[i] = block[half:].astype(BF16)
        for j in range(nu):
            block = (
                jnp.dot(
                    weighted[j * span : (j + 1) * span], picked(ccol[j, i]),
                    preferred_element_type=F32,
                )
                * scale
            )
            own_c[j, i] = block[: span // 2]
            xc_out[i, j] = block[span // 2 :].astype(BF16)
        return carry

    crossing = []
    per = rows // xd_s.shape[0]
    for g in range(xd_s.shape[0]):
        if g * per % size == 0:
            for e in peers:
                mu_part(g * per // size, e).wait_recv()
        lax.fori_loop(g * per, (g + 1) * per, sums_of, 0, unroll=True)
        part = pl.ds(g * per, per)
        crossing.append(
            (
                send(xd_out.at[part], xd_in.at[part], xd_s.at[g], xd_r.at[g], side),
                send(xc_out.at[part], xc_in.at[part], xc_s.at[g], xc_r.at[g], side),
            )
        )
    for copy in arriving:
        copy.wait_recv()
    total = share(r)
    for d in peers:
        total += inbox[0, d - 1].astype(F32)
    from_prev.wait_recv()
    back = jnp.where(tm > 0, defect_weight, 0.0)
    gshoot[...] = total + back * (start[...].astype(F32) - before[...].astype(F32))
    for copy in partial_in:
        copy.wait_recv()
    grads = igt[...] + igin[0] + igin[1] + igin[2]
    grads = jnp.concatenate([grads, jnp.zeros((width - scen, width), F32)], 0).T
    grads = grads * (blocks * width) ** (-0.5)
    for k in range(steps):
        gctl[k] = grads[k * nu : (k + 1) * nu, :scen]
    for one, two in crossing:
        one.wait_recv()
        two.wait_recv()
    for copy in pending:
        copy.wait_send()
    for k in range(steps):
        gather_whole(k, 1).wait_send()
        for g in range(chunks):
            gather_part(k, g, 2).wait_send()
            if k > 0 and g + 1 < chunks:
                gather_on(k, g).wait_send()
        if k > 0:
            gather_part(k, chunks - 1, 3).wait_send()
        else:
            gather_whole(k, 3).wait_send()
        for e in (1, 2):
            if k > 0:
                mu_copy(k, e).wait_send()
            line_copy(k, e).wait_send()
        pl.when(inner)(line_copy(k, 3).wait_send)
        pl.when(inner)(line_on(k).wait_send)
        for e in peers:
            over_y(k, e).wait_send()
            for h in range(2):
                over_core(k, e, h).wait_send()
        if k > 0:
            pl.when(inner)(mu_copy(k, 3).wait_send)
            pl.when(inner)(mu_on(k).wait_send)
    for g in range(chunks):
        for e in peers:
            mu_part(g, e).wait_send()


def finish_kernel(own_d, xd_in, own_c, xc_in, shoot_in, ctl_in, gdrift, gcontrol, gshoot, gctl):
    rows, half, _ = own_d.shape
    nu, deep, tile = xc_in.shape[1], xc_in.shape[2], 8

    def whole(i, carry):
        group, within = i // tile, lax.rem(i, tile)
        gdrift[pl.ds(group * (half * tile) + within, half, stride=tile), :] = own_d[i] + xd_in[
            i
        ].astype(F32)
        for j in range(nu):
            at = (j * (rows // tile) + group) * (deep * tile) + within
            gcontrol[pl.ds(at, deep, stride=tile), :] = own_c[j, i] + xc_in[i, j].astype(F32)
        return carry

    lax.fori_loop(0, rows, whole, 0, unroll=8)
    gshoot[...] = shoot_in[...]
    gctl[...] = ctl_in[...]


def shards(
    drift_blocks, drift_cols, control_blocks, control_cols, controls, shooting_states, targets
):
    group_count, row_count = lax.axis_size("tm"), lax.axis_size("rows")
    rows, slots, width, _ = drift_blocks.shape
    nu = control_blocks.shape[0]
    steps, scen, local = targets.shape
    if not (
        group_count == 2 * slots and slots == 4 and nu == 4 and row_count == 4 and steps == 5
        and scen == 8 and width == 128 and rows == 32
    ):
        return general(
            drift_blocks, drift_cols, control_blocks, control_cols, controls, shooting_states,
            targets,
        )
    blocks = rows * row_count
    pairs = group_count // 2
    first = jnp.swapaxes(shooting_states[0].reshape(scen, rows, width), 0, 1)
    tgt = jnp.swapaxes(targets.reshape(steps, scen, rows, width), 1, 2)
    ctl = jnp.swapaxes(controls, 0, 1)
    cols = jnp.swapaxes(drift_cols, 0, 1)
    span = width // slots
    count = rows * (slots + nu)
    vmem = pl.BlockSpec(memory_space=pltpu.VMEM)
    smem = pl.BlockSpec(memory_space=pltpu.SMEM)
    anywhere = pl.BlockSpec(memory_space=pl.ANY)
    dma = pltpu.SemaphoreType.DMA
    groups = 8
    panel = (rows, scen, width)
    gshoot, gctl, own_d, own_c, xd_in, xc_in = pl.pallas_call(
        sweep_kernel,
        out_shape=(
            pltpu.VMEM(panel, F32),
            pltpu.VMEM((steps, nu, scen), F32),
            pltpu.VMEM((rows, width // 2, width), F32),
            pltpu.VMEM((nu, rows, span // 2, width), F32),
            pltpu.VMEM((rows, width // 2, width), BF16),
            pltpu.VMEM((rows, nu, span // 2, width), BF16),
        ),
        in_specs=[smem, smem, vmem, vmem, anywhere, anywhere, vmem, vmem, vmem],
        out_specs=(vmem,) * 6,
        scratch_shapes=[
            *[pltpu.VMEM((blocks, scen, width), BF16) for _ in range(5)],
            pltpu.VMEM((steps, pairs - 1, blocks, scen, width), BF16),
            pltpu.VMEM((steps, pairs, rows, scen, width), BF16),
            pltpu.VMEM((scen * count, width), F32),
            pltpu.VMEM((blocks * scen, width), F32),
            pltpu.VMEM((steps, 3, rows, scen, width), BF16),
            pltpu.VMEM((steps, 3, rows, scen, width), BF16),
            pltpu.VMEM(panel, F32),
            pltpu.VMEM(panel, BF16),
            pltpu.VMEM(panel, BF16),
            pltpu.VMEM(panel, BF16),
            pltpu.VMEM((steps, nu, scen, width), F32),
            pltpu.VMEM((blocks, count), BF16),
            pltpu.VMEM((scen, width), F32),
            pltpu.VMEM((3, scen, width), F32),
            pltpu.VMEM((steps, scen, width), F32),
            pltpu.VMEM((3, steps, scen, width), F32),
            pltpu.VMEM((width, steps * pairs * scen), F32),
            pltpu.VMEM((2 * width, width), BF16),
            pltpu.VMEM((rows, width // 2, width), BF16),
            pltpu.VMEM((rows, nu, span // 2, width), BF16),
            pltpu.VMEM(drift_blocks.shape, BF16),
            pltpu.VMEM(control_blocks.shape, BF16),
            pltpu.VMEM((rows, (slots + nu) * width, width), BF16),
            dma((4,)), dma((nu,)),
            dma((steps, 3)), dma((steps, 3)),
            dma((steps, 4)), dma((steps, 4)), dma((steps, 4)),
            dma((steps, 3)), dma((steps, 3)), dma((steps,)),
            dma((steps, 3)), dma((steps, 3)),
            dma((steps, 3, 2)), dma((steps, 3, 2)),
            dma((steps, 3)), dma((steps, 3)), dma((steps,)), dma((4, 3)), dma((4, 3)),
            dma((steps, 3)), dma((steps, 3)),
            dma((3,)), dma((3,)),
            dma((3,)), dma((3,)),
            dma((2,)), dma((2,)),
            dma((groups,)), dma((groups,)),
            dma((groups,)), dma((groups,)),
        ],
        compiler_params=pltpu.CompilerParams(
            collective_id=0, has_side_effects=True, vmem_limit_bytes=52 * 2**20
        ),
        name="sweep",
    )(cols, control_cols, cols, control_cols, drift_blocks, control_blocks, ctl, first, tgt)

    gdrift, gcontrol, gshoot, gctl = pl.pallas_call(
        finish_kernel,
        out_shape=(
            jax.ShapeDtypeStruct((rows * width // 2, width), F32),
            jax.ShapeDtypeStruct((nu * rows * span // 2, width), F32),
            jax.ShapeDtypeStruct(panel, F32),
            jax.ShapeDtypeStruct((steps, nu, scen), F32),
        ),
        in_specs=[vmem] * 6,
        out_specs=(vmem,) * 4,
        name="finish",
    )(*[pltpu.with_memory_space_constraint(v, pltpu.VMEM) for v in (own_d, xd_in, own_c, xc_in, gshoot, gctl)])

    grad_shooting = jnp.swapaxes(gshoot, 0, 1).reshape(1, scen, local)
    grad_drift = gdrift.reshape(rows // 8, width // 2, 8, width)
    grad_control = gcontrol.reshape(nu, rows // 8, span // 2, 8, width)
    return (
        grad_shooting,
        jnp.swapaxes(gctl, 0, 1),
        jnp.swapaxes(grad_drift, 1, 2).reshape(rows, -1),
        jnp.swapaxes(grad_control, 2, 3).reshape(nu, rows, -1),
    )


def solution(mesh):
    return jax.shard_map(
        shards,
        mesh=mesh,
        in_specs=(
            P("rows", None, None, None),
            P("rows", None),
            P(None, "rows", None, None),
            P(None, "rows"),
            P(None, "tm", None),
            P("tm", None, "rows"),
            P("tm", None, "rows"),
        ),
        out_specs=(
            P("tm", None, "rows"),
            P(None, "tm", None),
            P("rows", "tm"),
            P(None, "rows", "tm"),
        ),
        check_vma=False,
    )
```
